512 devices in a mesh: gx: 32 (over y_hi, z, core), yz: 16 (over x, y_lo).
Axes of the slice: x: 4, y: 8 (y_hi: 2, y_lo: 4; y = y_hi * 4 + y_lo), z: 8, core: 2. Of those that a mesh axis runs over, the one named last changes fastest.
Arguments:
- gauge_links: float32 [64, 2, 3, 3, 2048], P('gx', None, None, None, 'yz'), may hold values from -1 to 1, as said below
- in_field: float32 [8, 64, 2, 3, 3, 2048], P(None, 'gx', None, None, None, 'yz'), may hold values from -6 to 6
- cotangent: float32 [8, 64, 2, 3, 3, 2048], P(None, 'gx', None, None, None, 'yz'), may hold values from -6 to 6
- bilinear_weights: float32 [8, 8, 24, 8], replicated, may hold values from -0.15625 to 0.15625
Outputs:
- grad_field: float32 [8, 64, 2, 3, 3, 2048], P(None, 'gx', None, None, None, 'yz')
- grad_weights: float32 [8, 8, 24, 8], replicated
The draws below stay inside these ranges and needn't reach their ends.
Inputs may be any that keep to these rules, and one draw needn't show every extreme that they name: `gauge_links`: every site's link is a special unitary 3 x 3 matrix (unitary with determinant 1), stored as real and imaginary parts.
All inputs are finite; a program needn't handle non-finite values.
Results may differ from the reference program's by a relative error of at most 0.0003.
Values sent between devices are 32-bit elements; how exact they have to be, the bound alone decides.
No kernel may reach another device: no remote copies, remote signals or barrier semaphores. Data moves between devices by JAX's collectives and lax.ppermute only.
A program may use at most 64 MiB of HBM per device.

```python
import jax
import jax.numpy as jnp
from jax import lax

C = 8
SDEV = 128
X = 64
S = 2048
LMAX = 24
N_YZ = 16


def rotation_pair(alpha, beta, gamma, first, second):
    zeros = jnp.zeros(alpha.shape, jnp.float32)
    ones = jnp.ones(alpha.shape, jnp.float32)
    cos_a = jnp.cos(alpha)
    sin_a = jnp.sin(alpha)
    real_rows = [[ones, zeros, zeros], [zeros, ones, zeros], [zeros, zeros, ones]]
    imag_rows = [[zeros, zeros, zeros], [zeros, zeros, zeros], [zeros, zeros, zeros]]
    real_rows[first][first] = cos_a * jnp.cos(beta)
    imag_rows[first][first] = cos_a * jnp.sin(beta)
    real_rows[first][second] = sin_a * jnp.cos(gamma)
    imag_rows[first][second] = sin_a * jnp.sin(gamma)
    real_rows[second][first] = -sin_a * jnp.cos(gamma)
    imag_rows[second][first] = sin_a * jnp.sin(gamma)
    real_rows[second][second] = cos_a * jnp.cos(beta)
    imag_rows[second][second] = -cos_a * jnp.sin(beta)
    real_part = jnp.stack([jnp.stack(row, axis=0) for row in real_rows], axis=0)
    imag_part = jnp.stack([jnp.stack(row, axis=0) for row in imag_rows], axis=0)
    return (real_part, imag_part)


def small_product(left_re, left_im, right_re, right_im):
    real_part = jnp.sum(left_re[:, :, None] * right_re[None, :, :], axis=1) - jnp.sum(left_im[:, :, None] * right_im[None, :, :], axis=1)
    imag_part = jnp.sum(left_re[:, :, None] * right_im[None, :, :], axis=1) + jnp.sum(left_im[:, :, None] * right_re[None, :, :], axis=1)
    return (real_part, imag_part)


def draw_gauge_links(key, part):
    base_key = jax.random.fold_in(key, 11)
    angles = jax.random.uniform(base_key, (11, X, S), jnp.float32, -3.14159, 3.14159)
    result_re, result_im = rotation_pair(angles[0], angles[1], angles[2], 0, 1)
    for index, (first, second) in enumerate(((1, 2), (0, 1))):
        step_re, step_im = rotation_pair(angles[3 + 3 * index], angles[4 + 3 * index], angles[5 + 3 * index], first, second)
        result_re, result_im = small_product(result_re, result_im, step_re, step_im)
    phase_one = angles[9]
    phase_two = angles[10]
    phase_three = -(phase_one + phase_two)
    phase_re = jnp.stack([jnp.cos(phase_one), jnp.cos(phase_two), jnp.cos(phase_three)], axis=0)
    phase_im = jnp.stack([jnp.sin(phase_one), jnp.sin(phase_two), jnp.sin(phase_three)], axis=0)
    final_re = result_re * phase_re[None] - result_im * phase_im[None]
    final_im = result_re * phase_im[None] + result_im * phase_re[None]
    matrices = jnp.stack([final_re, final_im], axis=0)
    return jnp.moveaxis(matrices, 3, 0).astype(jnp.float32)


def shard_levels(key, dims, split, least, top_value):
    factor_of = 1.0
    for position, parts in split:
        draws = jax.random.uniform(jax.random.fold_in(jax.random.fold_in(key, 6), position), (parts,), jnp.float32, least / len(split), top_value / len(split))
        factor_of = factor_of * jnp.repeat(jnp.exp(draws), dims[position] // parts).reshape((-1,) + (1,) * (len(dims) - 1 - position))
    return factor_of


def scatter_about(rng, shape, deviation, reach, split=(), kind=jnp.bfloat16):
    drawn = deviation * jax.random.normal(rng, shape, jnp.float32)
    if split:
        drawn = drawn * shard_levels(rng, shape, split, -0.22, 0.18)
    return jnp.clip(drawn, -reach, reach).astype(kind)


def setup_inputs(seed: int = 0) -> dict:
    key_list = jax.random.split(jax.random.key(seed), 5)
    gauge_links = draw_gauge_links(jax.random.fold_in(key_list[4], 71), 0)
    in_field = scatter_about(key_list[1], (C, X, 2, 3, 3, S), 1.0, 6.0, ((1, 32), (5, 16)), jnp.float32)
    cotangent = scatter_about(key_list[2], (C, X, 2, 3, 3, S), 1.0, 6.0, ((1, 32), (5, 16)), jnp.float32)
    bilinear_weights = scatter_about(key_list[3], (C, C, LMAX, C), (LMAX * C * C) ** -0.5, 0.15625, (), jnp.float32)
    return dict(gauge_links=gauge_links, in_field=in_field, cotangent=cotangent, bilinear_weights=bilinear_weights)


def matmul_three(left, right):
    return lax.optimization_barrier(jnp.sum(left[..., :, :, None, :] * right[..., None, :, :, :], axis=-3))

def complex_mul(left, right):
    left_re = left[..., 0, :, :, :]
    left_im = left[..., 1, :, :, :]
    right_re = right[..., 0, :, :, :]
    right_im = right[..., 1, :, :, :]
    real_part = matmul_three(left_re, right_re) - matmul_three(left_im, right_im)
    imag_part = matmul_three(left_re, right_im) + matmul_three(left_im, right_re)
    return jnp.stack([real_part, imag_part], axis=-4)

def dagger(matrix):
    swapped = jnp.swapaxes(matrix, -3, -2)
    return jnp.stack([swapped[..., 0, :, :, :], -swapped[..., 1, :, :, :]], axis=-4)

def reference(gauge_links, in_field, cotangent, bilinear_weights):
    weight_rows = bilinear_weights.reshape(C * C, LMAX * C)
    highest = lax.Precision.HIGHEST

    def one_block(block):
        block_links, block_field, block_cot = block
        pair_grad = complex_mul(dagger(block_field)[None], block_cot[:, None]).reshape(C * C, -1)
        line = block_links
        mixed = jnp.zeros((C * C, pair_grad.shape[1]), jnp.float32)
        transport_grad = jnp.zeros(block_field.shape, jnp.float32)
        pieces = []
        for offset in range(1, LMAX + 1):
            moved = jnp.roll(block_field, -offset, axis=1)
            transported = complex_mul(complex_mul(line[None], moved), dagger(line)[None])
            flat = transported.reshape(C, -1)
            weight_part = weight_rows[:, (offset - 1) * C:offset * C]
            mixed = mixed + jnp.dot(weight_part, flat, precision=highest)
            pieces.append(jnp.dot(pair_grad, flat.T, precision=highest))
            line_grad = jnp.dot(weight_part.T, pair_grad, precision=highest).reshape(block_field.shape)
            back_term = complex_mul(complex_mul(dagger(line)[None], line_grad), line[None])
            transport_grad = transport_grad + jnp.roll(back_term, offset, axis=1)
            line = complex_mul(line, jnp.roll(block_links, -offset, axis=0))
        mixed_matrix = mixed.reshape((C, C) + block_field.shape[1:])
        direct = lax.optimization_barrier(jnp.sum(complex_mul(block_cot[:, None], dagger(mixed_matrix)), axis=0))
        return (direct + transport_grad, jnp.concatenate(pieces, axis=1))
    links_blocks = jnp.moveaxis(gauge_links.reshape(X, 2, 3, 3, N_YZ, SDEV), 4, 0)
    field_blocks = jnp.moveaxis(in_field.reshape(C, X, 2, 3, 3, N_YZ, SDEV), 5, 0)
    cot_blocks = jnp.moveaxis(cotangent.reshape(C, X, 2, 3, 3, N_YZ, SDEV), 5, 0)
    grads, partials = lax.map(one_block, (links_blocks, field_blocks, cot_blocks))
    grad_field = jnp.moveaxis(grads, 0, 5).reshape(C, X, 2, 3, 3, S)
    grad_weights = lax.optimization_barrier(jnp.sum(partials, axis=0)).reshape(C, C, LMAX, C) / jnp.sqrt(100.0 * X * S)
    return (grad_field, grad_weights)
```

```python
import functools
import math

import jax
import jax.numpy as jnp
from jax import lax
from jax.experimental import pallas as pl
from jax.experimental.pallas import tpu as pltpu
from jax.sharding import PartitionSpec as P

C = 8
HALF = 320
HIGHEST = lax.Precision.HIGHEST


def comp(ri, a, b):
    return (ri * 3 + a) * 3 + b


def product(left, right, dag_left=False, dag_right=False):
    result = [None] * 18
    for a in range(3):
        for b in range(3):
            real = imag = None
            for k in range(3):
                l_at = (k, a) if dag_left else (a, k)
                r_at = (b, k) if dag_right else (k, b)
                l_re, l_im = left[comp(0, *l_at)], left[comp(1, *l_at)]
                r_re, r_im = right[comp(0, *r_at)], right[comp(1, *r_at)]
                rr, ii = l_re * r_re, l_im * r_im
                ri, ir = l_re * r_im, l_im * r_re
                term_re = rr + ii if dag_left != dag_right else rr - ii
                if not dag_left and not dag_right:
                    term_im = ri + ir
                elif dag_left and not dag_right:
                    term_im = ri - ir
                elif dag_right and not dag_left:
                    term_im = ir - ri
                else:
                    term_im = -(ri + ir)
                real = term_re if real is None else real + term_re
                imag = term_im if imag is None else imag + term_im
            result[comp(0, a, b)] = real
            result[comp(1, a, b)] = imag
    return result


def pack_kernel(links, field, cot, out, rows):
    rows[...] = jnp.zeros_like(rows)
    for x in range(2):
        base = x * HALF
        for ri in range(2):
            for a in range(3):
                first = comp(ri, a, 0)
                rows[pl.ds(base + 288 + first, 3), :] = links[x, ri, a]
                for c in range(C):
                    rows[pl.ds(base + first * 8 + c, 3, stride=8), :] = field[c, x, ri, a]
                    rows[pl.ds(base + 144 + first * 8 + c, 3, stride=8), :] = cot[c, x, ri, a]
    for block in range(5):
        turned = rows[pl.ds(128 * block, 128), :].T
        out[:, :, pl.ds(128 * block, 128)] = turned.reshape(32, 4, 128)


def layer_kernel(lines, packed, weights, grad_out, gw_out, rows, frame, wt, wp, gt, pair, windows, mixed, back, acc):
    shape = (C, 128)
    lane = lax.broadcasted_iota(jnp.int32, shape, 1)
    for block in range(5):
        turned = packed[:, :, pl.ds(128 * block, 128)].reshape(128, 128)
        rows[pl.ds(128 * block, 128), :] = turned.T

    def load8(x, offset):
        return [rows[pl.ds(x * HALF + offset + 8 * k, 8), :] for k in range(18)]

    def load_link(x):
        return [jnp.broadcast_to(rows[pl.ds(x * HALF + 288 + k, 1), :], shape) for k in range(18)]

    one = [jnp.full(shape, 1.0 if k in (0, 4, 8) else 0.0, jnp.float32) for k in range(18)]
    even = load_link(0)
    scan = product(even, load_link(1))
    step = 1
    while step < 32:
        moved = [pltpu.roll(v, 4 * step, 1) for v in scan]
        longer = product(moved, scan)
        scan = [jnp.where(lane >= 4 * step, n, v) for n, v in zip(longer, scan)]
        step *= 2
    for k in range(18):
        before = jnp.where(lane >= 4, pltpu.roll(scan[k], 4, 1), one[k])
        frame[0, k] = before
        whole = scan[k]
        reach = 1
        while reach < 32:
            whole = jnp.where(lane < 128 - 4 * reach, pltpu.roll(whole, 128 - 4 * reach, 1), whole)
            reach *= 2
        frame[2, k] = whole
    v_odd = product([frame[0, k] for k in range(18)], load_link(0))
    for k in range(18):
        frame[1, k] = v_odd[k]

    def get_frame(which):
        return [frame[which, k] for k in range(18)]

    for x in range(2):
        for offset, target in ((0, wt), (144, gt)):
            turned = product(product(get_frame(x), load8(x, offset)), get_frame(x), dag_right=True)
            for k in range(18):
                target[x, k] = turned[k]
        turned = product(product(get_frame(2), [wt[x, k] for k in range(18)]), get_frame(2), dag_right=True)
        for k in range(18):
            wp[x, k] = turned[k]

    for k in range(18):
        columns = pl.ds(128 * k, 128)
        for t in range(lines + 1):
            x, m = (t + 1) % 2, (t + 1) // 2
            value = wt[x, k]
            if m:
                value = pltpu.roll(jnp.where(lane < 4 * m, wp[x, k], value), 128 - 4 * m, 1)
            windows[pl.ds(8 * t, 8), columns] = value

    def spread(x, i):
        return [jnp.broadcast_to(gt[x, k, pl.ds(i, 1), :], shape) for k in range(18)]

    for x in range(2):
        @pl.loop(0, C)
        def _(i):
            value = product([wt[x, k] for k in range(18)], spread(x, i), dag_left=True)
            for k in range(18):
                pair[pl.ds(pl.multiple_of(64 * x + 8 * i, 8), 8), pl.ds(128 * k, 128)] = value[k]

    gw2 = lax.dot_general(pair[...], windows[...], (((1,), (1,)), ((), ())), precision=HIGHEST,
                          preferred_element_type=jnp.float32)
    width = lines * C
    gw_out[...] = gw2[:64, :width] + gw2[64:, 8:8 + width]

    mixed[...] = jnp.dot(weights[...], windows[...], precision=HIGHEST, preferred_element_type=jnp.float32)
    back[...] = lax.dot_general(weights[...], pair[...], (((0,), (0,)), ((), ())), precision=HIGHEST,
                                preferred_element_type=jnp.float32)

    for k in range(18):
        columns = pl.ds(128 * k, 128)
        for x in range(2):
            inside = jnp.zeros(shape, jnp.float32)
            wrapped = jnp.zeros(shape, jnp.float32)
            for t in range(lines + 1):
                if (t + 1) % 2 != x:
                    continue
                m = (t + 1) // 2
                value = back[pl.ds(8 * t, 8), columns]
                if m:
                    value = pltpu.roll(value, 4 * m, 1)
                    wrapped = wrapped + jnp.where(lane < 4 * m, value, 0.0)
                    inside = inside + jnp.where(lane < 4 * m, 0.0, value)
                else:
                    inside = inside + value
            acc[x, k] = inside
            wp[x, k] = wrapped

    for x in range(2):
        turned = product(product(get_frame(2), [wp[x, k] for k in range(18)], dag_left=True), get_frame(2))
        for k in range(18):
            acc[x, k] = acc[x, k] + turned[k]

        @pl.loop(0, C)
        def _(i):
            here = [mixed[pl.ds(pl.multiple_of(64 * x + 8 * i, 8), 8), pl.ds(128 * k, 128)] for k in range(18)]
            value = product(spread(x, i), here, dag_right=True)
            for k in range(18):
                acc[x, k] = acc[x, k] + value[k]

        turned = product(product(get_frame(x), [acc[x, k] for k in range(18)], dag_left=True), get_frame(x))
        for k in range(18):
            rows[pl.ds(144 * x + 8 * k, 8), :] = turned[k]
    rows[pl.ds(288, 96), :] = jnp.zeros((96, 128), jnp.float32)
    for block in range(3):
        turned = rows[pl.ds(128 * block, 128), :].T
        grad_out[:, :, pl.ds(128 * block, 128)] = turned.reshape(32, 4, 128)


def unpack_kernel(packed, out, rows):
    for block in range(3):
        turned = packed[:, :, pl.ds(128 * block, 128)].reshape(128, 128)
        rows[pl.ds(128 * block, 128), :] = turned.T
    for x in range(2):
        for ri in range(2):
            for a in range(3):
                for c in range(C):
                    out[c, x, ri, a] = rows[pl.ds(144 * x + comp(ri, a, 0) * 8 + c, 3, stride=8), :]


def per_device(gauge_links, in_field, cotangent, bilinear_weights):
    lines = bilinear_weights.shape[2]
    width = lines * C
    f32 = jnp.float32
    n_gx, n_yz = lax.axis_size("gx"), lax.axis_size("yz")
    flat = bilinear_weights.reshape(C * C, width)
    weights = jnp.concatenate([jnp.pad(flat, ((0, 0), (0, 8))), jnp.pad(flat, ((0, 0), (8, 0)))], axis=0)
    vmem = lambda *shape: pltpu.VMEM(shape, f32)
    packed = pl.pallas_call(
        pack_kernel,
        out_shape=jax.ShapeDtypeStruct((32, 4, 640), f32),
        scratch_shapes=[vmem(640, 128)],
        name="pack",
    )(gauge_links, in_field, cotangent)
    packed = lax.all_to_all(packed, "gx", 0, 0, tiled=True)
    wide = 18 * 128
    grad_part, gw_part = pl.pallas_call(
        functools.partial(layer_kernel, lines),
        out_shape=(jax.ShapeDtypeStruct((32, 4, 384), f32), jax.ShapeDtypeStruct((64, width), f32)),
        scratch_shapes=[
            vmem(640, 128),
            vmem(3, 18, 8, 128),
            vmem(2, 18, 8, 128),
            vmem(2, 18, 8, 128),
            vmem(2, 18, 8, 128),
            vmem(128, wide),
            vmem(width + 8, wide),
            vmem(128, wide),
            vmem(width + 8, wide),
            vmem(2, 18, 8, 128),
        ],
        name="layer",
    )(packed, weights)
    gw_part = lax.all_to_all(gw_part.reshape(n_yz, 64 // n_yz, width), "yz", 0, 0, tiled=True)
    gw_part = jnp.sum(gw_part, axis=0)
    both = jnp.concatenate([grad_part[:, :, :288], jnp.broadcast_to(gw_part[None], (n_gx,) + gw_part.shape)], axis=2)
    both = lax.all_to_all(both, "gx", 0, 0, tiled=True)
    total = jnp.sum(both[:, :, 288:], axis=0)
    scale = 1.0 / math.sqrt(100.0 * 2 * n_gx * 128 * n_yz)
    total = jnp.broadcast_to((total * scale)[None], (n_yz,) + total.shape)
    grad_weights = lax.all_to_all(total, "yz", 0, 0, tiled=True).reshape(C, C, lines, C)
    back = jnp.pad(both[:, :, :288], ((0, 0), (0, 0), (0, 96)))
    grad_field = pl.pallas_call(
        unpack_kernel,
        out_shape=jax.ShapeDtypeStruct(in_field.shape, f32),
        scratch_shapes=[vmem(384, 128)],
        name="unpack",
    )(back)
    return (grad_field, grad_weights)


def solution(mesh):
    placed = (
        P("gx", None, None, None, "yz"),
        P(None, "gx", None, None, None, "yz"),
        P(None, "gx", None, None, None, "yz"),
        P(),
    )
    return jax.shard_map(
        per_device,
        mesh=mesh,
        in_specs=placed,
        out_specs=(P(None, "gx", None, None, None, "yz"), P()),
        check_vma=False,
    )
```

```python
import functools
import math

import jax
import jax.numpy as jnp
from jax import lax
from jax.experimental import pallas as pl
from jax.experimental.pallas import tpu as pltpu
from jax.sharding import PartitionSpec as P

C = 8
HALF = 320
HIGHEST = lax.Precision.HIGHEST


def comp(ri, a, b):
    return (a * 3 + b) * 2 + ri


def product(left, right, dag_left=False, dag_right=False):
    result = [None] * 18
    for a in range(3):
        for b in range(3):
            real = imag = None
            for k in range(3):
                l_at = (k, a) if dag_left else (a, k)
                r_at = (b, k) if dag_right else (k, b)
                l_re, l_im = left[comp(0, *l_at)], left[comp(1, *l_at)]
                r_re, r_im = right[comp(0, *r_at)], right[comp(1, *r_at)]
                rr, ii = l_re * r_re, l_im * r_im
                ri, ir = l_re * r_im, l_im * r_re
                term_re = rr + ii if dag_left != dag_right else rr - ii
                if not dag_left and not dag_right:
                    term_im = ri + ir
                elif dag_left and not dag_right:
                    term_im = ri - ir
                elif dag_right and not dag_left:
                    term_im = ir - ri
                else:
                    term_im = -(ri + ir)
                real = term_re if real is None else real + term_re
                imag = term_im if imag is None else imag + term_im
            result[comp(0, a, b)] = real
            result[comp(1, a, b)] = imag
    return result


def pack_kernel(links, field, cot, out, rows):
    for x in range(2):
        base = x * HALF
        for k in range(18):
            rows[pl.ds(base + 8 * k, 8), :] = field[pl.ds(18 * x + k, C, stride=36), :]
            rows[pl.ds(base + 144 + 8 * k, 8), :] = cot[pl.ds(18 * x + k, C, stride=36), :]
        for k in range(9):
            rows[pl.ds(base + 288 + 2 * k, 2), :] = links[x, k // 3, k % 3]
        rows[pl.ds(base + 306, 14), :] = jnp.zeros((14, 128), jnp.float32)
    for block in range(5):
        turned = rows[pl.ds(128 * block, 128), :].T
        out[:, :, pl.ds(128 * block, 128)] = turned.reshape(32, 4, 128)


def layer_kernel(lines, packed, weights, grad_out, gw_out, rows, frame, wt, wp, gt, pair, windows, mixed, back, acc):
    shape = (C, 128)
    lane = lax.broadcasted_iota(jnp.int32, shape, 1)
    for block in range(5):
        turned = packed[:, :, pl.ds(128 * block, 128)].reshape(128, 128)
        rows[pl.ds(128 * block, 128), :] = turned.T

    def load8(x, offset):
        return [rows[pl.ds(x * HALF + offset + 8 * k, 8), :] for k in range(18)]

    def load_link(x):
        return [jnp.broadcast_to(rows[pl.ds(x * HALF + 288 + k, 1), :], shape) for k in range(18)]

    one = [jnp.full(shape, 1.0 if k in (0, 8, 16) else 0.0, jnp.float32) for k in range(18)]
    even = load_link(0)
    scan = product(even, load_link(1))
    step = 1
    while step < 32:
        moved = [pltpu.roll(v, 4 * step, 1) for v in scan]
        longer = product(moved, scan)
        scan = [jnp.where(lane >= 4 * step, n, v) for n, v in zip(longer, scan)]
        step *= 2
    for k in range(18):
        before = jnp.where(lane >= 4, pltpu.roll(scan[k], 4, 1), one[k])
        frame[0, k] = before
        whole = scan[k]
        reach = 1
        while reach < 32:
            whole = jnp.where(lane < 128 - 4 * reach, pltpu.roll(whole, 128 - 4 * reach, 1), whole)
            reach *= 2
        frame[2, k] = whole
    v_odd = product([frame[0, k] for k in range(18)], load_link(0))
    for k in range(18):
        frame[1, k] = v_odd[k]

    def get_frame(which):
        return [frame[which, k] for k in range(18)]

    for x in range(2):
        for offset, target in ((0, wt), (144, gt)):
            turned = product(product(get_frame(x), load8(x, offset)), get_frame(x), dag_right=True)
            for k in range(18):
                target[x, k] = turned[k]
        turned = product(product(get_frame(2), [wt[x, k] for k in range(18)]), get_frame(2), dag_right=True)
        for k in range(18):
            wp[x, k] = turned[k]

    for k in range(18):
        columns = pl.ds(128 * k, 128)
        for t in range(lines + 1):
            x, m = (t + 1) % 2, (t + 1) // 2
            value = wt[x, k]
            if m:
                value = pltpu.roll(jnp.where(lane < 4 * m, wp[x, k], value), 128 - 4 * m, 1)
            windows[pl.ds(8 * t, 8), columns] = value

    def spread(x, i):
        return [jnp.broadcast_to(gt[x, k, pl.ds(i, 1), :], shape) for k in range(18)]

    for x in range(2):
        @pl.loop(0, C)
        def _(i):
            value = product([wt[x, k] for k in range(18)], spread(x, i), dag_left=True)
            for k in range(18):
                pair[pl.ds(pl.multiple_of(64 * x + 8 * i, 8), 8), pl.ds(128 * k, 128)] = value[k]

    gw2 = lax.dot_general(pair[...], windows[...], (((1,), (1,)), ((), ())), precision=HIGHEST,
                          preferred_element_type=jnp.float32)
    width = lines * C
    gw_out[...] = gw2[:64, :width] + gw2[64:, 8:8 + width]

    mixed[...] = jnp.dot(weights[...], windows[...], precision=HIGHEST, preferred_element_type=jnp.float32)
    back[...] = lax.dot_general(weights[...], pair[...], (((0,), (0,)), ((), ())), precision=HIGHEST,
                                preferred_element_type=jnp.float32)

    for k in range(18):
        columns = pl.ds(128 * k, 128)
        for x in range(2):
            inside = jnp.zeros(shape, jnp.float32)
            wrapped = jnp.zeros(shape, jnp.float32)
            for t in range(lines + 1):
                if (t + 1) % 2 != x:
                    continue
                m = (t + 1) // 2
                value = back[pl.ds(8 * t, 8), columns]
                if m:
                    value = pltpu.roll(value, 4 * m, 1)
                    wrapped = wrapped + jnp.where(lane < 4 * m, value, 0.0)
                    inside = inside + jnp.where(lane < 4 * m, 0.0, value)
                else:
                    inside = inside + value
            acc[x, k] = inside
            wp[x, k] = wrapped

    for x in range(2):
        turned = product(product(get_frame(2), [wp[x, k] for k in range(18)], dag_left=True), get_frame(2))
        for k in range(18):
            acc[x, k] = acc[x, k] + turned[k]

        @pl.loop(0, C)
        def _(i):
            here = [mixed[pl.ds(pl.multiple_of(64 * x + 8 * i, 8), 8), pl.ds(128 * k, 128)] for k in range(18)]
            value = product(spread(x, i), here, dag_right=True)
            for k in range(18):
                acc[x, k] = acc[x, k] + value[k]

        turned = product(product(get_frame(x), [acc[x, k] for k in range(18)], dag_left=True), get_frame(x))
        for k in range(18):
            rows[pl.ds(144 * x + 8 * k, 8), :] = turned[k]
    rows[pl.ds(288, 96), :] = jnp.zeros((96, 128), jnp.float32)
    for block in range(3):
        turned = rows[pl.ds(128 * block, 128), :].T
        grad_out[:, :, pl.ds(128 * block, 128)] = turned.reshape(32, 4, 128)


def unpack_kernel(packed, out, rows):
    for block in range(3):
        turned = packed[:, :, pl.ds(128 * block, 128)].reshape(128, 128)
        rows[pl.ds(128 * block, 128), :] = turned.T
    for x in range(2):
        for k in range(18):
            out[pl.ds(18 * x + k, C, stride=36), :] = rows[pl.ds(144 * x + 8 * k, 8), :]


def per_device(gauge_links, in_field, cotangent, bilinear_weights):
    lines = bilinear_weights.shape[2]
    width = lines * C
    f32 = jnp.float32
    n_gx, n_yz = lax.axis_size("gx"), lax.axis_size("yz")
    flat = bilinear_weights.reshape(C * C, width)
    weights = jnp.concatenate([jnp.pad(flat, ((0, 0), (0, 8))), jnp.pad(flat, ((0, 0), (8, 0)))], axis=0)
    vmem = lambda *shape: pltpu.VMEM(shape, f32)
    grant = lambda mib: pltpu.CompilerParams(vmem_limit_bytes=mib << 20)
    as_rows = lambda v: jnp.transpose(v, (0, 1, 3, 4, 2, 5)).reshape(-1, 128)
    packed = pl.pallas_call(
        pack_kernel,
        out_shape=jax.ShapeDtypeStruct((32, 4, 640), f32),
        scratch_shapes=[vmem(640, 128)],
        compiler_params=grant(4),
        name="pack",
    )(jnp.transpose(gauge_links, (0, 2, 3, 1, 4)), as_rows(in_field), as_rows(cotangent))
    packed = lax.all_to_all(packed, "gx", 0, 0, tiled=True)
    wide = 18 * 128
    grad_part, gw_part = pl.pallas_call(
        functools.partial(layer_kernel, lines),
        out_shape=(jax.ShapeDtypeStruct((32, 4, 384), f32), jax.ShapeDtypeStruct((64, width), f32)),
        scratch_shapes=[
            vmem(640, 128),
            vmem(3, 18, 8, 128),
            vmem(2, 18, 8, 128),
            vmem(2, 18, 8, 128),
            vmem(2, 18, 8, 128),
            vmem(128, wide),
            vmem(width + 8, wide),
            vmem(128, wide),
            vmem(width + 8, wide),
            vmem(2, 18, 8, 128),
        ],
        compiler_params=grant(14),
        name="layer",
    )(packed, weights)
    gw_part = lax.all_to_all(gw_part.reshape(n_yz, 64 // n_yz, width), "yz", 0, 0, tiled=True)
    gw_part = jnp.sum(gw_part, axis=0)
    both = jnp.concatenate([grad_part[:, :, :288], jnp.broadcast_to(gw_part[None], (n_gx,) + gw_part.shape)], axis=2)
    both = lax.all_to_all(both, "gx", 0, 0, tiled=True)
    total = jnp.sum(both[:, :, 288:], axis=0)
    scale = 1.0 / math.sqrt(100.0 * 2 * n_gx * 128 * n_yz)
    total = jnp.broadcast_to((total * scale)[None], (n_yz,) + total.shape)
    grad_weights = lax.all_to_all(total, "yz", 0, 0, tiled=True).reshape(C, C, lines, C)
    back = jnp.pad(both[:, :, :288], ((0, 0), (0, 0), (0, 96)))
    grad_field = pl.pallas_call(
        unpack_kernel,
        out_shape=jax.ShapeDtypeStruct((288, 128), f32),
        scratch_shapes=[vmem(384, 128)],
        compiler_params=grant(4),
        name="unpack",
    )(back)
    grad_field = jnp.transpose(grad_field.reshape(C, 2, 3, 3, 2, 128), (0, 1, 4, 2, 3, 5))
    return (grad_field, grad_weights)


def solution(mesh):
    placed = (
        P("gx", None, None, None, "yz"),
        P(None, "gx", None, None, None, "yz"),
        P(None, "gx", None, None, None, "yz"),
        P(),
    )
    return jax.shard_map(
        per_device,
        mesh=mesh,
        in_specs=placed,
        out_specs=(P(None, "gx", None, None, None, "yz"), P()),
        check_vma=False,
    )
```

```python
import functools
import math

import jax
import jax.numpy as jnp
from jax import lax
from jax.experimental import pallas as pl
from jax.experimental.pallas import tpu as pltpu
from jax.sharding import PartitionSpec as P

C = 8
HALF = 320
HIGHEST = lax.Precision.HIGHEST


def comp(ri, a, b):
    return (a * 3 + b) * 2 + ri


def product(left, right, dag_left=False, dag_right=False):
    result = [None] * 18
    for a in range(3):
        for b in range(3):
            real = imag = None
            for k in range(3):
                l_at = (k, a) if dag_left else (a, k)
                r_at = (b, k) if dag_right else (k, b)
                l_re, l_im = left[comp(0, *l_at)], left[comp(1, *l_at)]
                r_re, r_im = right[comp(0, *r_at)], right[comp(1, *r_at)]
                rr, ii = l_re * r_re, l_im * r_im
                ri, ir = l_re * r_im, l_im * r_re
                term_re = rr + ii if dag_left != dag_right else rr - ii
                if not dag_left and not dag_right:
                    term_im = ri + ir
                elif dag_left and not dag_right:
                    term_im = ri - ir
                elif dag_right and not dag_left:
                    term_im = ir - ri
                else:
                    term_im = -(ri + ir)
                real = term_re if real is None else real + term_re
                imag = term_im if imag is None else imag + term_im
            result[comp(0, a, b)] = real
            result[comp(1, a, b)] = imag
    return result


def pack_kernel(links, field, cot, out, rows):
    for x in range(2):
        base = x * HALF
        for k in range(18):
            rows[pl.ds(base + 8 * k, 8), :] = field[pl.ds(18 * x + k, C, stride=36), :]
            rows[pl.ds(base + 144 + 8 * k, 8), :] = cot[pl.ds(18 * x + k, C, stride=36), :]
        for k in range(9):
            rows[pl.ds(base + 288 + 2 * k, 2), :] = links[x, k // 3, k % 3]
        rows[pl.ds(base + 306, 14), :] = jnp.zeros((14, 128), jnp.float32)
    for block in range(5):
        turned = rows[pl.ds(128 * block, 128), :].T
        out[:, :, pl.ds(128 * block, 128)] = turned.reshape(32, 4, 128)


KEPT = (128, 24, 16, 16, 16)


def parts_of(state):
    starts = [sum(KEPT[:n]) for n in range(len(KEPT))]
    return [state.at[pl.ds(start, size), :] for start, size in zip(starts, KEPT)]


def tile(ref, which, k):
    return ref[pl.ds(8 * which, 8), pl.ds(128 * k, 128)]


def put(ref, which, k, value):
    ref[pl.ds(8 * which, 8), pl.ds(128 * k, 128)] = value


def fill_windows(lines, wt, wp, windows):
    lane = lax.broadcasted_iota(jnp.int32, (C, 128), 1)
    for k in range(18):
        for t in range(lines + 1):
            x, m = (t + 1) % 2, (t + 1) // 2
            value = tile(wt, x, k)
            if m:
                value = pltpu.roll(jnp.where(lane < 4 * m, tile(wp, x, k), value), 128 - 4 * m, 1)
            put(windows, t, k, value)


def forward_kernel(lines, packed, gw_out, state, rows, gt, windows):
    pair, frame, gt_kept, wt, wp = parts_of(state)
    shape = (C, 128)
    lane = lax.broadcasted_iota(jnp.int32, shape, 1)
    for block in range(5):
        turned = packed[:, :, pl.ds(128 * block, 128)].reshape(128, 128)
        rows[pl.ds(128 * block, 128), :] = turned.T

    def load8(x, offset):
        return [rows[pl.ds(x * HALF + offset + 8 * k, 8), :] for k in range(18)]

    def load_link(x):
        return [jnp.broadcast_to(rows[pl.ds(x * HALF + 288 + k, 1), :], shape) for k in range(18)]

    one = [jnp.full(shape, 1.0 if k in (0, 8, 16) else 0.0, jnp.float32) for k in range(18)]
    even = load_link(0)
    scan = product(even, load_link(1))
    step = 1
    while step < 32:
        moved = [pltpu.roll(v, 4 * step, 1) for v in scan]
        longer = product(moved, scan)
        scan = [jnp.where(lane >= 4 * step, n, v) for n, v in zip(longer, scan)]
        step *= 2
    for k in range(18):
        before = jnp.where(lane >= 4, pltpu.roll(scan[k], 4, 1), one[k])
        put(frame, 0, k, before)
        whole = scan[k]
        reach = 1
        while reach < 32:
            whole = jnp.where(lane < 128 - 4 * reach, pltpu.roll(whole, 128 - 4 * reach, 1), whole)
            reach *= 2
        put(frame, 2, k, whole)
    def get_frame(which):
        return [tile(frame, which, k) for k in range(18)]

    v_odd = product(get_frame(0), load_link(0))
    for k in range(18):
        put(frame, 1, k, v_odd[k])

    for x in range(2):
        turned = product(product(get_frame(x), load8(x, 144)), get_frame(x), dag_right=True)
        for k in range(18):
            put(gt_kept, x, k, turned[k])
            gt[x, k] = turned[k]
        turned = product(product(get_frame(x), load8(x, 0)), get_frame(x), dag_right=True)
        for k in range(18):
            put(wt, x, k, turned[k])
        turned = product(product(get_frame(2), [tile(wt, x, k) for k in range(18)]), get_frame(2), dag_right=True)
        for k in range(18):
            put(wp, x, k, turned[k])

    fill_windows(lines, wt, wp, windows)

    for x in range(2):
        @pl.loop(0, C)
        def _(i):
            value = product([tile(wt, x, k) for k in range(18)], spread(gt, x, i), dag_left=True)
            for k in range(18):
                pair[pl.ds(pl.multiple_of(64 * x + 8 * i, 8), 8), pl.ds(128 * k, 128)] = value[k]

    gw2 = lax.dot_general(pair[...], windows[...], (((1,), (1,)), ((), ())), precision=HIGHEST,
                          preferred_element_type=jnp.float32)
    width = lines * C
    gw_out[...] = (gw2[:64, :width] + gw2[64:, 8:8 + width]).reshape(gw_out.shape)


def spread(source, x, i):
    return [jnp.broadcast_to(source[x, k, pl.ds(i, 1), :], (C, 128)) for k in range(18)]


def backward_kernel(lines, weights, state, grad_out, rows, mixed, back, acc, wrap, gt, windows):
    pair, frame, gt_kept, wt, wp = parts_of(state)
    fill_windows(lines, wt, wp, windows)
    for x in range(2):
        for k in range(18):
            gt[x, k] = tile(gt_kept, x, k)
    shape = (C, 128)
    lane = lax.broadcasted_iota(jnp.int32, shape, 1)

    def get_frame(which):
        return [tile(frame, which, k) for k in range(18)]

    mixed[...] = jnp.dot(weights[...], windows[...], precision=HIGHEST, preferred_element_type=jnp.float32)
    back[...] = lax.dot_general(weights[...], pair[...], (((0,), (0,)), ((), ())), precision=HIGHEST,
                                preferred_element_type=jnp.float32)

    for k in range(18):
        columns = pl.ds(128 * k, 128)
        for x in range(2):
            inside = jnp.zeros(shape, jnp.float32)
            wrapped = jnp.zeros(shape, jnp.float32)
            for t in range(lines + 1):
                if (t + 1) % 2 != x:
                    continue
                m = (t + 1) // 2
                value = back[pl.ds(8 * t, 8), columns]
                if m:
                    value = pltpu.roll(value, 4 * m, 1)
                    wrapped = wrapped + jnp.where(lane < 4 * m, value, 0.0)
                    inside = inside + jnp.where(lane < 4 * m, 0.0, value)
                else:
                    inside = inside + value
            acc[x, k] = inside
            wrap[x, k] = wrapped

    for x in range(2):
        turned = product(product(get_frame(2), [wrap[x, k] for k in range(18)], dag_left=True), get_frame(2))
        for k in range(18):
            acc[x, k] = acc[x, k] + turned[k]

        @pl.loop(0, C)
        def _(i):
            here = [mixed[pl.ds(pl.multiple_of(64 * x + 8 * i, 8), 8), pl.ds(128 * k, 128)] for k in range(18)]
            value = product(spread(gt, x, i), here, dag_right=True)
            for k in range(18):
                acc[x, k] = acc[x, k] + value[k]

        turned = product(product(get_frame(x), [acc[x, k] for k in range(18)], dag_left=True), get_frame(x))
        for k in range(18):
            rows[pl.ds(144 * x + 8 * k, 8), :] = turned[k]
    rows[pl.ds(288, 96), :] = jnp.zeros((96, 128), jnp.float32)
    for block in range(3):
        turned = rows[pl.ds(128 * block, 128), :].T
        grad_out[:, :, pl.ds(128 * block, 128)] = turned.reshape(32, 4, 128)


def unpack_kernel(packed, out, rows):
    for block in range(3):
        turned = packed[:, :, pl.ds(128 * block, 128)].reshape(128, 128)
        rows[pl.ds(128 * block, 128), :] = turned.T
    for x in range(2):
        for k in range(18):
            out[pl.ds(18 * x + k, C, stride=36), :] = rows[pl.ds(144 * x + 8 * k, 8), :]


def per_device(gauge_links, in_field, cotangent, bilinear_weights):
    lines = bilinear_weights.shape[2]
    width = lines * C
    f32 = jnp.float32
    n_gx, n_yz = lax.axis_size("gx"), lax.axis_size("yz")
    flat = bilinear_weights.reshape(C * C, width)
    weights = jnp.concatenate([jnp.pad(flat, ((0, 0), (0, 8))), jnp.pad(flat, ((0, 0), (8, 0)))], axis=0)
    vmem = lambda *shape: pltpu.VMEM(shape, f32)
    grant = lambda mib: pltpu.CompilerParams(vmem_limit_bytes=mib << 20)
    as_rows = lambda v: jnp.transpose(v, (0, 1, 3, 4, 2, 5)).reshape(-1, 128)
    packed = pl.pallas_call(
        pack_kernel,
        out_shape=jax.ShapeDtypeStruct((32, 4, 640), f32),
        scratch_shapes=[vmem(640, 128)],
        compiler_params=grant(4),
        name="pack",
    )(jnp.transpose(gauge_links, (0, 2, 3, 1, 4)), as_rows(in_field), as_rows(cotangent))
    packed = lax.all_to_all(packed, "gx", 0, 0, tiled=True)
    wide = 18 * 128
    shapes = lambda *dims: jax.ShapeDtypeStruct(dims, f32)
    gw_part, state = pl.pallas_call(
        functools.partial(forward_kernel, lines),
        out_shape=(
            shapes(n_yz, 64 // n_yz, width),
            shapes(sum(KEPT), wide),
        ),
        scratch_shapes=[vmem(640, 128), vmem(2, 18, 8, 128), vmem(width + 8, wide)],
        compiler_params=grant(12),
        cost_estimate=pl.CostEstimate(flops=10**9, bytes_accessed=4 << 20, transcendentals=0),
        name="forward",
    )(packed)
    grad_part = pl.pallas_call(
        functools.partial(backward_kernel, lines),
        out_shape=shapes(32, 4, 384),
        scratch_shapes=[
            vmem(384, 128),
            vmem(128, wide),
            vmem(width + 8, wide),
            vmem(2, 18, 8, 128),
            vmem(2, 18, 8, 128),
            vmem(2, 18, 8, 128),
            vmem(width + 8, wide),
        ],
        compiler_params=grant(14),
        cost_estimate=pl.CostEstimate(flops=2 * 10**9, bytes_accessed=4 << 20, transcendentals=0),
        name="backward",
    )(weights, state)
    gw_part = lax.all_to_all(gw_part, "yz", 0, 0, tiled=True)
    gw_part = jnp.sum(gw_part, axis=0)
    both = jnp.concatenate([grad_part[:, :, :288], jnp.broadcast_to(gw_part[None], (n_gx,) + gw_part.shape)], axis=2)
    both = lax.all_to_all(both, "gx", 0, 0, tiled=True)
    total = jnp.sum(both[:, :, 288:], axis=0)
    scale = 1.0 / math.sqrt(100.0 * 2 * n_gx * 128 * n_yz)
    total = jnp.broadcast_to((total * scale)[None], (n_yz,) + total.shape)
    grad_weights = lax.all_to_all(total, "yz", 0, 0, tiled=True).reshape(C, C, lines, C)
    back = jnp.pad(both[:, :, :288], ((0, 0), (0, 0), (0, 96)))
    grad_field = pl.pallas_call(
        unpack_kernel,
        out_shape=jax.ShapeDtypeStruct((288, 128), f32),
        scratch_shapes=[vmem(384, 128)],
        compiler_params=grant(4),
        name="unpack",
    )(back)
    grad_field = jnp.transpose(grad_field.reshape(C, 2, 3, 3, 2, 128), (0, 1, 4, 2, 3, 5))
    return (grad_field, grad_weights)


def solution(mesh):
    placed = (
        P("gx", None, None, None, "yz"),
        P(None, "gx", None, None, None, "yz"),
        P(None, "gx", None, None, None, "yz"),
        P(),
    )
    return jax.shard_map(
        per_device,
        mesh=mesh,
        in_specs=placed,
        out_specs=(P(None, "gx", None, None, None, "yz"), P()),
        check_vma=False,
    )
```

```python
import functools
import math

import jax
import jax.numpy as jnp
from jax import lax
from jax.experimental import pallas as pl
from jax.experimental.pallas import tpu as pltpu
from jax.sharding import PartitionSpec as P

C = 8
WHOLE = 67043328
HALF = 320


def comp(ri, a, b):
    return (a * 3 + b) * 2 + ri


def product(left, right, dag_left=False, dag_right=False):
    result = [None] * 18
    for a in range(3):
        for b in range(3):
            real = imag = None
            for k in range(3):
                l_at = (k, a) if dag_left else (a, k)
                r_at = (b, k) if dag_right else (k, b)
                l_re, l_im = left[comp(0, *l_at)], left[comp(1, *l_at)]
                r_re, r_im = right[comp(0, *r_at)], right[comp(1, *r_at)]
                rr, ii = l_re * r_re, l_im * r_im
                ri, ir = l_re * r_im, l_im * r_re
                term_re = rr + ii if dag_left != dag_right else rr - ii
                if not dag_left and not dag_right:
                    term_im = ri + ir
                elif dag_left and not dag_right:
                    term_im = ri - ir
                elif dag_right and not dag_left:
                    term_im = ir - ri
                else:
                    term_im = -(ri + ir)
                real = term_re if real is None else real + term_re
                imag = term_im if imag is None else imag + term_im
            result[comp(0, a, b)] = real
            result[comp(1, a, b)] = imag
    return result


def halves(value):
    high = value.astype(jnp.bfloat16)
    return high, (value - high.astype(jnp.float32)).astype(jnp.bfloat16)


def matmul(left, right, dims):
    left_high, left_low = halves(left)
    right_high, right_low = halves(right)
    dot = functools.partial(lax.dot_general, dimension_numbers=(dims, ((), ())), preferred_element_type=jnp.float32)
    return dot(left_high, right_high) + (dot(left_low, right_high) + dot(left_high, right_low))


def pack_kernel(links_far, field_far, cot_far, out, links, field, cot, rows, sems):
    copies = [
        pltpu.make_async_copy(far, near, sems.at[n])
        for n, (far, near) in enumerate(((field_far, field), (links_far, links), (cot_far, cot)))
    ]
    for copy in copies:
        copy.start()
    copies[0].wait()
    for x in range(2):
        rows[pl.ds(x * HALF + 306, 14), :] = jnp.zeros((14, 128), jnp.float32)
        for k in range(18):
            rows[pl.ds(x * HALF + 8 * k, 8), :] = field[pl.ds(18 * x + k, C, stride=36), :]
    copies[1].wait()
    for x in range(2):
        for k in range(9):
            rows[pl.ds(x * HALF + 288 + 2 * k, 2), :] = links[x, k // 3, k % 3]
    copies[2].wait()
    for x in range(2):
        for k in range(18):
            rows[pl.ds(x * HALF + 144 + 8 * k, 8), :] = cot[pl.ds(18 * x + k, C, stride=36), :]
    for block in range(5):
        turned = rows[pl.ds(128 * block, 128), :].T
        out[:, :, pl.ds(128 * block, 128)] = turned.reshape(32, 4, 128)


KEPT = (128, 24, 16, 16, 16)


def parts_of(state):
    starts = [sum(KEPT[:n]) for n in range(len(KEPT))]
    return [state.at[pl.ds(start, size), :] for start, size in zip(starts, KEPT)]


def tile(ref, which, k):
    return ref[pl.ds(8 * which, 8), pl.ds(128 * k, 128)]


def put(ref, which, k, value):
    ref[pl.ds(8 * which, 8), pl.ds(128 * k, 128)] = value


def fill_windows(lines, wt, wp, windows):
    lane = lax.broadcasted_iota(jnp.int32, (C, 128), 1)
    for k in range(18):
        for t in range(lines + 1):
            x, m = (t + 1) % 2, (t + 1) // 2
            value = tile(wt, x, k)
            if m:
                value = pltpu.roll(jnp.where(lane < 4 * m, tile(wp, x, k), value), 128 - 4 * m, 1)
            put(windows, t, k, value)


def forward_kernel(lines, packed, gw_out, state, rows, gt, windows):
    pair, frame, gt_kept, wt, wp = parts_of(state)
    shape = (C, 128)
    lane = lax.broadcasted_iota(jnp.int32, shape, 1)
    for block in range(5):
        turned = packed[:, :, pl.ds(128 * block, 128)].reshape(128, 128)
        rows[pl.ds(128 * block, 128), :] = turned.T

    def load8(x, offset):
        return [rows[pl.ds(x * HALF + offset + 8 * k, 8), :] for k in range(18)]

    def load_link(x):
        return [jnp.broadcast_to(rows[pl.ds(x * HALF + 288 + k, 1), :], shape) for k in range(18)]

    one = [jnp.full(shape, 1.0 if k in (0, 8, 16) else 0.0, jnp.float32) for k in range(18)]
    even = load_link(0)
    scan = product(even, load_link(1))
    step = 1
    while step < 32:
        moved = [pltpu.roll(v, 4 * step, 1) for v in scan]
        longer = product(moved, scan)
        scan = [jnp.where(lane >= 4 * step, n, v) for n, v in zip(longer, scan)]
        step *= 2
    for k in range(18):
        before = jnp.where(lane >= 4, pltpu.roll(scan[k], 4, 1), one[k])
        put(frame, 0, k, before)
        whole = scan[k]
        reach = 1
        while reach < 32:
            whole = jnp.where(lane < 128 - 4 * reach, pltpu.roll(whole, 128 - 4 * reach, 1), whole)
            reach *= 2
        put(frame, 2, k, whole)
    def get_frame(which):
        return [tile(frame, which, k) for k in range(18)]

    v_odd = product(get_frame(0), load_link(0))
    for k in range(18):
        put(frame, 1, k, v_odd[k])

    for x in range(2):
        turned = product(product(get_frame(x), load8(x, 144)), get_frame(x), dag_right=True)
        for k in range(18):
            put(gt_kept, x, k, turned[k])
            gt[x, k] = turned[k]
        turned = product(product(get_frame(x), load8(x, 0)), get_frame(x), dag_right=True)
        for k in range(18):
            put(wt, x, k, turned[k])
        turned = product(product(get_frame(2), [tile(wt, x, k) for k in range(18)]), get_frame(2), dag_right=True)
        for k in range(18):
            put(wp, x, k, turned[k])

    fill_windows(lines, wt, wp, windows)

    for x in range(2):
        @pl.loop(0, C)
        def _(i):
            value = product([tile(wt, x, k) for k in range(18)], spread(gt, x, i), dag_left=True)
            for k in range(18):
                pair[pl.ds(pl.multiple_of(64 * x + 8 * i, 8), 8), pl.ds(128 * k, 128)] = value[k]

    gw2 = matmul(pair[...], windows[...], ((1,), (1,)))
    width = lines * C
    gw_out[...] = (gw2[:64, :width] + gw2[64:, 8:8 + width]).reshape(gw_out.shape)


def spread(source, x, i):
    return [jnp.broadcast_to(source[x, k, pl.ds(i, 1), :], (C, 128)) for k in range(18)]


def backward_kernel(lines, weights, state, grad_out, rows, mixed, back, acc, wrap, gt, windows):
    pair, frame, gt_kept, wt, wp = parts_of(state)
    fill_windows(lines, wt, wp, windows)
    for x in range(2):
        for k in range(18):
            gt[x, k] = tile(gt_kept, x, k)
    shape = (C, 128)
    lane = lax.broadcasted_iota(jnp.int32, shape, 1)

    def get_frame(which):
        return [tile(frame, which, k) for k in range(18)]

    mixed[...] = matmul(weights[...], windows[...], ((1,), (0,)))
    back[...] = matmul(weights[...], pair[...], ((0,), (0,)))

    for k in range(18):
        columns = pl.ds(128 * k, 128)
        for x in range(2):
            inside = jnp.zeros(shape, jnp.float32)
            wrapped = jnp.zeros(shape, jnp.float32)
            for t in range(lines + 1):
                if (t + 1) % 2 != x:
                    continue
                m = (t + 1) // 2
                value = back[pl.ds(8 * t, 8), columns]
                if m:
                    value = pltpu.roll(value, 4 * m, 1)
                    wrapped = wrapped + jnp.where(lane < 4 * m, value, 0.0)
                    inside = inside + jnp.where(lane < 4 * m, 0.0, value)
                else:
                    inside = inside + value
            acc[x, k] = inside
            wrap[x, k] = wrapped

    for x in range(2):
        turned = product(product(get_frame(2), [wrap[x, k] for k in range(18)], dag_left=True), get_frame(2))
        for k in range(18):
            acc[x, k] = acc[x, k] + turned[k]

        @pl.loop(0, C)
        def _(i):
            here = [mixed[pl.ds(pl.multiple_of(64 * x + 8 * i, 8), 8), pl.ds(128 * k, 128)] for k in range(18)]
            value = product(spread(gt, x, i), here, dag_right=True)
            for k in range(18):
                acc[x, k] = acc[x, k] + value[k]

        turned = product(product(get_frame(x), [acc[x, k] for k in range(18)], dag_left=True), get_frame(x))
        for k in range(18):
            rows[pl.ds(144 * x + 8 * k, 8), :] = turned[k]
    rows[pl.ds(288, 96), :] = jnp.zeros((96, 128), jnp.float32)
    for block in range(3):
        turned = rows[pl.ds(128 * block, 128), :].T
        grad_out[:, :, pl.ds(128 * block, 128)] = turned.reshape(32, 4, 128)


def unpack_kernel(packed, out, rows):
    for block in range(3):
        turned = packed[:, :, pl.ds(128 * block, 128)].reshape(128, 128)
        rows[pl.ds(128 * block, 128), :] = turned.T
    for x in range(2):
        for k in range(18):
            out[pl.ds(18 * x + k, C, stride=36), :] = rows[pl.ds(144 * x + 8 * k, 8), :]


def per_device(gauge_links, in_field, cotangent, bilinear_weights):
    lines = bilinear_weights.shape[2]
    width = lines * C
    f32 = jnp.float32
    n_gx, n_yz = lax.axis_size("gx"), lax.axis_size("yz")
    flat = bilinear_weights.reshape(C * C, width)
    weights = jnp.concatenate([jnp.pad(flat, ((0, 0), (0, 8))), jnp.pad(flat, ((0, 0), (8, 0)))], axis=0)
    vmem = lambda *shape: pltpu.VMEM(shape, f32)
    grant = lambda mib: pltpu.CompilerParams(vmem_limit_bytes=mib << 20)
    as_rows = lambda v: jnp.transpose(v, (0, 1, 3, 4, 2, 5)).reshape(-1, 128)
    packed = pl.pallas_call(
        pack_kernel,
        out_shape=jax.ShapeDtypeStruct((32, 4, 640), f32),
        in_specs=[pl.BlockSpec(memory_space=pltpu.HBM)] * 3,
        scratch_shapes=[
            vmem(2, 3, 3, 2, 128),
            vmem(288, 128),
            vmem(288, 128),
            vmem(640, 128),
            pltpu.SemaphoreType.DMA((3,)),
        ],
        compiler_params=pltpu.CompilerParams(vmem_limit_bytes=WHOLE),
        name="pack",
    )(jnp.transpose(gauge_links, (0, 2, 3, 1, 4)), as_rows(in_field), as_rows(cotangent))
    packed = lax.all_to_all(packed, "gx", 0, 0, tiled=True)
    wide = 18 * 128
    shapes = lambda *dims: jax.ShapeDtypeStruct(dims, f32)
    gw_part, state = pl.pallas_call(
        functools.partial(forward_kernel, lines),
        out_shape=(
            shapes(n_yz, 64 // n_yz, width),
            shapes(sum(KEPT), wide),
        ),
        scratch_shapes=[vmem(640, 128), vmem(2, 18, 8, 128), vmem(width + 8, wide)],
        compiler_params=grant(12),
        cost_estimate=pl.CostEstimate(flops=10**9, bytes_accessed=4 << 20, transcendentals=0),
        name="forward",
    )(packed)
    grad_part = pl.pallas_call(
        functools.partial(backward_kernel, lines),
        out_shape=shapes(32, 4, 384),
        scratch_shapes=[
            vmem(384, 128),
            vmem(128, wide),
            vmem(width + 8, wide),
            vmem(2, 18, 8, 128),
            vmem(2, 18, 8, 128),
            vmem(2, 18, 8, 128),
            vmem(width + 8, wide),
        ],
        compiler_params=grant(14),
        cost_estimate=pl.CostEstimate(flops=2 * 10**9, bytes_accessed=4 << 20, transcendentals=0),
        name="backward",
    )(weights, state)
    gw_part = lax.all_to_all(gw_part, "yz", 0, 0, tiled=True)
    gw_part = jnp.sum(gw_part, axis=0)
    both = jnp.concatenate([grad_part[:, :, :288], jnp.broadcast_to(gw_part[None], (n_gx,) + gw_part.shape)], axis=2)
    both = lax.all_to_all(both, "gx", 0, 0, tiled=True)
    total = jnp.sum(both[:, :, 288:], axis=0)
    scale = 1.0 / math.sqrt(100.0 * 2 * n_gx * 128 * n_yz)
    total = jnp.broadcast_to((total * scale)[None], (n_yz,) + total.shape)
    grad_weights = lax.all_to_all(total, "yz", 0, 0, tiled=True).reshape(C, C, lines, C)
    back = jnp.pad(both[:, :, :288], ((0, 0), (0, 0), (0, 96)))
    grad_field = pl.pallas_call(
        unpack_kernel,
        out_shape=jax.ShapeDtypeStruct((288, 128), f32),
        scratch_shapes=[vmem(384, 128)],
        compiler_params=grant(4),
        name="unpack",
    )(back)
    grad_field = jnp.transpose(grad_field.reshape(C, 2, 3, 3, 2, 128), (0, 1, 4, 2, 3, 5))
    return (grad_field, grad_weights)


def solution(mesh):
    placed = (
        P("gx", None, None, None, "yz"),
        P(None, "gx", None, None, None, "yz"),
        P(None, "gx", None, None, None, "yz"),
        P(),
    )
    return jax.shard_map(
        per_device,
        mesh=mesh,
        in_specs=placed,
        out_specs=(P(None, "gx", None, None, None, "yz"), P()),
        check_vma=False,
    )
```

```python
import functools
import math

import jax
import jax.numpy as jnp
from jax import lax
from jax.experimental import pallas as pl
from jax.experimental.pallas import tpu as pltpu
from jax.sharding import PartitionSpec as P

C = 8
WHOLE = 67043328
HALF = 320


def comp(ri, a, b):
    return (a * 3 + b) * 2 + ri


def product(left, right, dag_left=False, dag_right=False):
    result = [None] * 18
    for a in range(3):
        for b in range(3):
            real = imag = None
            for k in range(3):
                l_at = (k, a) if dag_left else (a, k)
                r_at = (b, k) if dag_right else (k, b)
                l_re, l_im = left[comp(0, *l_at)], left[comp(1, *l_at)]
                r_re, r_im = right[comp(0, *r_at)], right[comp(1, *r_at)]
                rr, ii = l_re * r_re, l_im * r_im
                ri, ir = l_re * r_im, l_im * r_re
                term_re = rr + ii if dag_left != dag_right else rr - ii
                if not dag_left and not dag_right:
                    term_im = ri + ir
                elif dag_left and not dag_right:
                    term_im = ri - ir
                elif dag_right and not dag_left:
                    term_im = ir - ri
                else:
                    term_im = -(ri + ir)
                real = term_re if real is None else real + term_re
                imag = term_im if imag is None else imag + term_im
            result[comp(0, a, b)] = real
            result[comp(1, a, b)] = imag
    return result


def halves(value):
    high = value.astype(jnp.bfloat16)
    return high, (value - high.astype(jnp.float32)).astype(jnp.bfloat16)


def matmul(left, right, dims):
    left_high, left_low = halves(left)
    right_high, right_low = halves(right)
    dot = functools.partial(lax.dot_general, dimension_numbers=(dims, ((), ())), preferred_element_type=jnp.float32)
    return dot(left_high, right_high) + (dot(left_low, right_high) + dot(left_high, right_low))


def pack_kernel(links_far, field_far, cot_far, out, links, field, cot, rows, sems):
    copies = [
        pltpu.make_async_copy(far, near, sems.at[n])
        for n, (far, near) in enumerate(((field_far, field), (links_far, links), (cot_far, cot)))
    ]
    for copy in copies:
        copy.start()
    copies[0].wait()
    for x in range(2):
        rows[pl.ds(x * HALF + 306, 14), :] = jnp.zeros((14, 128), jnp.float32)
        for k in range(18):
            rows[pl.ds(x * HALF + 8 * k, 8), :] = field[pl.ds(18 * x + k, C, stride=36), :]
    copies[1].wait()
    for x in range(2):
        for k in range(9):
            rows[pl.ds(x * HALF + 288 + 2 * k, 2), :] = links[x, k // 3, k % 3]
    copies[2].wait()
    for x in range(2):
        for k in range(18):
            rows[pl.ds(x * HALF + 144 + 8 * k, 8), :] = cot[pl.ds(18 * x + k, C, stride=36), :]
    for block in range(5):
        turned = rows[pl.ds(128 * block, 128), :].T
        out[:, :, pl.ds(128 * block, 128)] = turned.reshape(32, 4, 128)


KEPT = (128, 24, 16, 16, 16)


def parts_of(state):
    starts = [sum(KEPT[:n]) for n in range(len(KEPT))]
    return [state.at[pl.ds(start, size), :] for start, size in zip(starts, KEPT)]


def tile(ref, which, k):
    return ref[pl.ds(8 * which, 8), pl.ds(128 * k, 128)]


def put(ref, which, k, value):
    ref[pl.ds(8 * which, 8), pl.ds(128 * k, 128)] = value


def fill_windows(lines, wt, wp, windows, entries=range(18)):
    lane = lax.broadcasted_iota(jnp.int32, (C, 128), 1)
    for k in entries:
        for t in range(lines + 1):
            x, m = (t + 1) % 2, (t + 1) // 2
            value = tile(wt, x, k)
            if m:
                value = pltpu.roll(jnp.where(lane < 4 * m, tile(wp, x, k), value), 128 - 4 * m, 1)
            put(windows, t, k, value)


def forward_kernel(lines, packed, gw_out, state, rows, gt, windows):
    pair, frame, gt_kept, wt, wp = parts_of(state)
    shape = (C, 128)
    lane = lax.broadcasted_iota(jnp.int32, shape, 1)
    for block in range(5):
        turned = packed[:, :, pl.ds(128 * block, 128)].reshape(128, 128)
        rows[pl.ds(128 * block, 128), :] = turned.T

    def load8(x, offset):
        return [rows[pl.ds(x * HALF + offset + 8 * k, 8), :] for k in range(18)]

    def load_link(x):
        return [jnp.broadcast_to(rows[pl.ds(x * HALF + 288 + k, 1), :], shape) for k in range(18)]

    one = [jnp.full(shape, 1.0 if k in (0, 8, 16) else 0.0, jnp.float32) for k in range(18)]
    even = load_link(0)
    scan = product(even, load_link(1))
    step = 1
    while step < 32:
        moved = [pltpu.roll(v, 4 * step, 1) for v in scan]
        longer = product(moved, scan)
        scan = [jnp.where(lane >= 4 * step, n, v) for n, v in zip(longer, scan)]
        step *= 2
    for k in range(18):
        before = jnp.where(lane >= 4, pltpu.roll(scan[k], 4, 1), one[k])
        put(frame, 0, k, before)
        whole = scan[k]
        reach = 1
        while reach < 32:
            whole = jnp.where(lane < 128 - 4 * reach, pltpu.roll(whole, 128 - 4 * reach, 1), whole)
            reach *= 2
        put(frame, 2, k, whole)
    def get_frame(which):
        return [tile(frame, which, k) for k in range(18)]

    v_odd = product(get_frame(0), load_link(0))
    for k in range(18):
        put(frame, 1, k, v_odd[k])

    for x in range(2):
        turned = product(product(get_frame(x), load8(x, 144)), get_frame(x), dag_right=True)
        for k in range(18):
            put(gt_kept, x, k, turned[k])
            gt[x, k] = turned[k]
        turned = product(product(get_frame(x), load8(x, 0)), get_frame(x), dag_right=True)
        for k in range(18):
            put(wt, x, k, turned[k])
        turned = product(product(get_frame(2), [tile(wt, x, k) for k in range(18)]), get_frame(2), dag_right=True)
        for k in range(18):
            put(wp, x, k, turned[k])

    for x in range(2):
        for i in range(C):
            value = product([tile(wt, x, k) for k in range(18)], spread(gt, x, i), dag_left=True)
            for k in range(18):
                put(pair, 8 * x + i, k, value[k])
    gw2 = None
    for first in range(0, 18, 2):
        fill_windows(lines, wt, wp, windows, range(first, first + 2))
        columns = pl.ds(128 * first, 128 * 2)
        part = matmul(pair[:, columns], windows[:, columns], ((1,), (1,)))
        gw2 = part if gw2 is None else gw2 + part
    width = lines * C
    gw_out[...] = (gw2[:64, :width] + gw2[64:, 8:8 + width]).reshape(gw_out.shape)


def spread(source, x, i):
    return [jnp.broadcast_to(source[x, k, pl.ds(i, 1), :], (C, 128)) for k in range(18)]


def backward_kernel(lines, weights, state, grad_out, rows, mixed, back, acc, wrap, gt, windows):
    pair, frame, gt_kept, wt, wp = parts_of(state)
    fill_windows(lines, wt, wp, windows)
    for x in range(2):
        for k in range(18):
            gt[x, k] = tile(gt_kept, x, k)
    shape = (C, 128)
    lane = lax.broadcasted_iota(jnp.int32, shape, 1)

    def get_frame(which):
        return [tile(frame, which, k) for k in range(18)]

    for first in range(0, 18, 6):
        columns = pl.ds(128 * first, 128 * 6)
        mixed[:, columns] = matmul(weights[...], windows[:, columns], ((1,), (0,)))
        back[:, columns] = matmul(weights[...], pair[:, columns], ((0,), (0,)))

    for k in range(18):
        columns = pl.ds(128 * k, 128)
        for x in range(2):
            inside = jnp.zeros(shape, jnp.float32)
            wrapped = jnp.zeros(shape, jnp.float32)
            for t in range(lines + 1):
                if (t + 1) % 2 != x:
                    continue
                m = (t + 1) // 2
                value = back[pl.ds(8 * t, 8), columns]
                if m:
                    value = pltpu.roll(value, 4 * m, 1)
                    wrapped = wrapped + jnp.where(lane < 4 * m, value, 0.0)
                    inside = inside + jnp.where(lane < 4 * m, 0.0, value)
                else:
                    inside = inside + value
            acc[x, k] = inside
            wrap[x, k] = wrapped

    for x in range(2):
        turned = product(product(get_frame(2), [wrap[x, k] for k in range(18)], dag_left=True), get_frame(2))
        for k in range(18):
            acc[x, k] = acc[x, k] + turned[k]

        for i in range(C):
            here = [tile(mixed, 8 * x + i, k) for k in range(18)]
            value = product(spread(gt, x, i), here, dag_right=True)
            for k in range(18):
                acc[x, k] = acc[x, k] + value[k]

        turned = product(product(get_frame(x), [acc[x, k] for k in range(18)], dag_left=True), get_frame(x))
        for k in range(18):
            rows[pl.ds(144 * x + 8 * k, 8), :] = turned[k]
    rows[pl.ds(288, 96), :] = jnp.zeros((96, 128), jnp.float32)
    for block in range(3):
        turned = rows[pl.ds(128 * block, 128), :].T
        grad_out[:, :, pl.ds(128 * block, 128)] = turned.reshape(32, 4, 128)


def unpack_kernel(packed, out, rows):
    for block in range(3):
        turned = packed[:, :, pl.ds(128 * block, 128)].reshape(128, 128)
        rows[pl.ds(128 * block, 128), :] = turned.T
    for x in range(2):
        for k in range(18):
            out[pl.ds(18 * x + k, C, stride=36), :] = rows[pl.ds(144 * x + 8 * k, 8), :]


def per_device(gauge_links, in_field, cotangent, bilinear_weights):
    lines = bilinear_weights.shape[2]
    width = lines * C
    f32 = jnp.float32
    n_gx, n_yz = lax.axis_size("gx"), lax.axis_size("yz")
    flat = bilinear_weights.reshape(C * C, width)
    weights = jnp.concatenate([jnp.pad(flat, ((0, 0), (0, 8))), jnp.pad(flat, ((0, 0), (8, 0)))], axis=0)
    vmem = lambda *shape: pltpu.VMEM(shape, f32)
    grant = lambda mib: pltpu.CompilerParams(vmem_limit_bytes=mib << 20)
    as_rows = lambda v: jnp.transpose(v, (0, 1, 3, 4, 2, 5)).reshape(-1, 128)
    packed = pl.pallas_call(
        pack_kernel,
        out_shape=jax.ShapeDtypeStruct((32, 4, 640), f32),
        in_specs=[pl.BlockSpec(memory_space=pltpu.HBM)] * 3,
        scratch_shapes=[
            vmem(2, 3, 3, 2, 128),
            vmem(288, 128),
            vmem(288, 128),
            vmem(640, 128),
            pltpu.SemaphoreType.DMA((3,)),
        ],
        compiler_params=pltpu.CompilerParams(vmem_limit_bytes=WHOLE),
        name="pack",
    )(jnp.transpose(gauge_links, (0, 2, 3, 1, 4)), as_rows(in_field), as_rows(cotangent))
    packed = lax.all_to_all(packed, "gx", 0, 0, tiled=True)
    wide = 18 * 128
    shapes = lambda *dims: jax.ShapeDtypeStruct(dims, f32)
    gw_part, state = pl.pallas_call(
        functools.partial(forward_kernel, lines),
        out_shape=(
            shapes(n_yz, 64 // n_yz, width),
            shapes(sum(KEPT), wide),
        ),
        scratch_shapes=[vmem(640, 128), vmem(2, 18, 8, 128), vmem(width + 8, wide)],
        compiler_params=grant(12),
        cost_estimate=pl.CostEstimate(flops=10**9, bytes_accessed=4 << 20, transcendentals=0),
        name="forward",
    )(packed)
    grad_part = pl.pallas_call(
        functools.partial(backward_kernel, lines),
        out_shape=shapes(32, 4, 384),
        scratch_shapes=[
            vmem(384, 128),
            vmem(128, wide),
            vmem(width + 8, wide),
            vmem(2, 18, 8, 128),
            vmem(2, 18, 8, 128),
            vmem(2, 18, 8, 128),
            vmem(width + 8, wide),
        ],
        compiler_params=grant(14),
        cost_estimate=pl.CostEstimate(flops=2 * 10**9, bytes_accessed=4 << 20, transcendentals=0),
        name="backward",
    )(weights, state)
    gw_part = lax.all_to_all(gw_part, "yz", 0, 0, tiled=True)
    gw_part = jnp.sum(gw_part, axis=0)
    both = jnp.concatenate([grad_part[:, :, :288], jnp.broadcast_to(gw_part[None], (n_gx,) + gw_part.shape)], axis=2)
    both = lax.all_to_all(both, "gx", 0, 0, tiled=True)
    total = jnp.sum(both[:, :, 288:], axis=0)
    scale = 1.0 / math.sqrt(100.0 * 2 * n_gx * 128 * n_yz)
    total = jnp.broadcast_to((total * scale)[None], (n_yz,) + total.shape)
    grad_weights = lax.all_to_all(total, "yz", 0, 0, tiled=True).reshape(C, C, lines, C)
    back = jnp.pad(both[:, :, :288], ((0, 0), (0, 0), (0, 96)))
    grad_field = pl.pallas_call(
        unpack_kernel,
        out_shape=jax.ShapeDtypeStruct((288, 128), f32),
        scratch_shapes=[vmem(384, 128)],
        compiler_params=grant(4),
        name="unpack",
    )(back)
    grad_field = jnp.transpose(grad_field.reshape(C, 2, 3, 3, 2, 128), (0, 1, 4, 2, 3, 5))
    return (grad_field, grad_weights)


def solution(mesh):
    placed = (
        P("gx", None, None, None, "yz"),
        P(None, "gx", None, None, None, "yz"),
        P(None, "gx", None, None, None, "yz"),
        P(),
    )
    return jax.shard_map(
        per_device,
        mesh=mesh,
        in_specs=placed,
        out_specs=(P(None, "gx", None, None, None, "yz"), P()),
        check_vma=False,
    )
```

```python
import functools
import math

import jax
import jax.numpy as jnp
from jax import lax
from jax.experimental import pallas as pl
from jax.experimental.pallas import tpu as pltpu
from jax.sharding import PartitionSpec as P

C = 8
WHOLE = 67043328
HALF = 320


def comp(ri, a, b):
    return (a * 3 + b) * 2 + ri


def product(left, right, dag_left=False, dag_right=False):
    result = [None] * 18
    for a in range(3):
        for b in range(3):
            real = imag = None
            for k in range(3):
                l_at = (k, a) if dag_left else (a, k)
                r_at = (b, k) if dag_right else (k, b)
                l_re, l_im = left[comp(0, *l_at)], left[comp(1, *l_at)]
                r_re, r_im = right[comp(0, *r_at)], right[comp(1, *r_at)]
                rr, ii = l_re * r_re, l_im * r_im
                ri, ir = l_re * r_im, l_im * r_re
                term_re = rr + ii if dag_left != dag_right else rr - ii
                if not dag_left and not dag_right:
                    term_im = ri + ir
                elif dag_left and not dag_right:
                    term_im = ri - ir
                elif dag_right and not dag_left:
                    term_im = ir - ri
                else:
                    term_im = -(ri + ir)
                real = term_re if real is None else real + term_re
                imag = term_im if imag is None else imag + term_im
            result[comp(0, a, b)] = real
            result[comp(1, a, b)] = imag
    return result


def halves(value):
    high = value.astype(jnp.bfloat16)
    return high, (value - high.astype(jnp.float32)).astype(jnp.bfloat16)


def matmul(left, right, dims):
    left_high, left_low = halves(left)
    right_high, right_low = halves(right)
    dot = functools.partial(lax.dot_general, dimension_numbers=(dims, ((), ())), preferred_element_type=jnp.float32)
    return dot(left_high, right_high) + (dot(left_low, right_high) + dot(left_high, right_low))


def pack_kernel(links_far, field_far, cot_far, out, links, field, cot, rows, sems):
    copies = [
        pltpu.make_async_copy(far, near, sems.at[n])
        for n, (far, near) in enumerate(((field_far, field), (links_far, links), (cot_far, cot)))
    ]
    for copy in copies:
        copy.start()
    copies[0].wait()
    for x in range(2):
        rows[pl.ds(x * HALF + 306, 14), :] = jnp.zeros((14, 128), jnp.float32)
        for k in range(18):
            rows[pl.ds(x * HALF + 8 * k, 8), :] = field[pl.ds(18 * x + k, C, stride=36), :]
    copies[1].wait()
    for x in range(2):
        for k in range(9):
            rows[pl.ds(x * HALF + 288 + 2 * k, 2), :] = links[x, k // 3, k % 3]
    copies[2].wait()
    for x in range(2):
        for k in range(18):
            rows[pl.ds(x * HALF + 144 + 8 * k, 8), :] = cot[pl.ds(18 * x + k, C, stride=36), :]
    for block in range(5):
        turned = rows[pl.ds(128 * block, 128), :].T
        out[:, :, pl.ds(128 * block, 128)] = turned.reshape(32, 4, 128)


KEPT = (128, 24, 16, 16)


def parts_of(state):
    starts = [sum(KEPT[:n]) for n in range(len(KEPT))]
    return [state.at[pl.ds(start, size), :] for start, size in zip(starts, KEPT)]


def tile(ref, which, k):
    return ref[pl.ds(8 * which, 8), pl.ds(128 * k, 128)]


def put(ref, which, k, value):
    ref[pl.ds(8 * which, 8), pl.ds(128 * k, 128)] = value


def fill_windows(lines, wt, wp, windows, entries=range(18)):
    lane = lax.broadcasted_iota(jnp.int32, (C, 128), 1)
    for k in entries:
        for t in range(lines + 1):
            x, m = (t + 1) % 2, (t + 1) // 2
            value = tile(wt, x, k)
            if m:
                value = pltpu.roll(jnp.where(lane < 4 * m, tile(wp, x, k), value), 128 - 4 * m, 1)
            put(windows, t, k, value)


def spread(source, x, i):
    return [jnp.broadcast_to(source[x, k, pl.ds(i, 1), :], (C, 128)) for k in range(18)]


def layer_kernel(lines, packed, weights, gw_out, grad_out, state, rows, gt, windows, mixed, back, acc, wrap):
    pair, frame, wt, wp = parts_of(state)
    shape = (C, 128)
    lane = lax.broadcasted_iota(jnp.int32, shape, 1)
    for block in range(5):
        turned = packed[:, :, pl.ds(128 * block, 128)].reshape(128, 128)
        rows[pl.ds(128 * block, 128), :] = turned.T

    def load8(x, offset):
        return [rows[pl.ds(x * HALF + offset + 8 * k, 8), :] for k in range(18)]

    def load_link(x):
        return [jnp.broadcast_to(rows[pl.ds(x * HALF + 288 + k, 1), :], shape) for k in range(18)]

    one = [jnp.full(shape, 1.0 if k in (0, 8, 16) else 0.0, jnp.float32) for k in range(18)]
    even = load_link(0)
    scan = product(even, load_link(1))
    step = 1
    while step < 32:
        moved = [pltpu.roll(v, 4 * step, 1) for v in scan]
        longer = product(moved, scan)
        scan = [jnp.where(lane >= 4 * step, n, v) for n, v in zip(longer, scan)]
        step *= 2
    for k in range(18):
        before = jnp.where(lane >= 4, pltpu.roll(scan[k], 4, 1), one[k])
        put(frame, 0, k, before)
        whole = scan[k]
        reach = 1
        while reach < 32:
            whole = jnp.where(lane < 128 - 4 * reach, pltpu.roll(whole, 128 - 4 * reach, 1), whole)
            reach *= 2
        put(frame, 2, k, whole)
    def get_frame(which):
        return [tile(frame, which, k) for k in range(18)]

    v_odd = product(get_frame(0), load_link(0))
    for k in range(18):
        put(frame, 1, k, v_odd[k])

    for x in range(2):
        turned = product(product(get_frame(x), load8(x, 144)), get_frame(x), dag_right=True)
        for k in range(18):
            gt[x, k] = turned[k]
        turned = product(product(get_frame(x), load8(x, 0)), get_frame(x), dag_right=True)
        for k in range(18):
            put(wt, x, k, turned[k])
        turned = product(product(get_frame(2), [tile(wt, x, k) for k in range(18)]), get_frame(2), dag_right=True)
        for k in range(18):
            put(wp, x, k, turned[k])

    for x in range(2):
        for i in range(C):
            value = product([tile(wt, x, k) for k in range(18)], spread(gt, x, i), dag_left=True)
            for k in range(18):
                put(pair, 8 * x + i, k, value[k])
    gw2 = None
    for first in range(0, 18, 2):
        fill_windows(lines, wt, wp, windows, range(first, first + 2))
        columns = pl.ds(128 * first, 128 * 2)
        part = matmul(pair[:, columns], windows[:, columns], ((1,), (1,)))
        gw2 = part if gw2 is None else gw2 + part
    width = lines * C
    gw_out[...] = (gw2[:64, :width] + gw2[64:, 8:8 + width]).reshape(gw_out.shape)

    for first in range(0, 18, 6):
        columns = pl.ds(128 * first, 128 * 6)
        mixed[:, columns] = matmul(weights[...], windows[:, columns], ((1,), (0,)))
        back[:, columns] = matmul(weights[...], pair[:, columns], ((0,), (0,)))

    for k in range(18):
        columns = pl.ds(128 * k, 128)
        for x in range(2):
            inside = jnp.zeros(shape, jnp.float32)
            wrapped = jnp.zeros(shape, jnp.float32)
            for t in range(lines + 1):
                if (t + 1) % 2 != x:
                    continue
                m = (t + 1) // 2
                value = back[pl.ds(8 * t, 8), columns]
                if m:
                    value = pltpu.roll(value, 4 * m, 1)
                    wrapped = wrapped + jnp.where(lane < 4 * m, value, 0.0)
                    inside = inside + jnp.where(lane < 4 * m, 0.0, value)
                else:
                    inside = inside + value
            acc[x, k] = inside
            wrap[x, k] = wrapped

    for x in range(2):
        turned = product(product(get_frame(2), [wrap[x, k] for k in range(18)], dag_left=True), get_frame(2))
        for k in range(18):
            acc[x, k] = acc[x, k] + turned[k]

        for i in range(C):
            here = [tile(mixed, 8 * x + i, k) for k in range(18)]
            value = product(spread(gt, x, i), here, dag_right=True)
            for k in range(18):
                acc[x, k] = acc[x, k] + value[k]

        turned = product(product(get_frame(x), [acc[x, k] for k in range(18)], dag_left=True), get_frame(x))
        for k in range(18):
            rows[pl.ds(144 * x + 8 * k, 8), :] = turned[k]
    rows[pl.ds(288, 96), :] = jnp.zeros((96, 128), jnp.float32)
    for block in range(3):
        turned = rows[pl.ds(128 * block, 128), :].T
        grad_out[:, :, pl.ds(128 * block, 128)] = turned.reshape(32, 4, 128)


def unpack_kernel(packed, out, rows):
    for block in range(3):
        turned = packed[:, :, pl.ds(128 * block, 128)].reshape(128, 128)
        rows[pl.ds(128 * block, 128), :] = turned.T
    for x in range(2):
        for k in range(18):
            out[pl.ds(18 * x + k, C, stride=36), :] = rows[pl.ds(144 * x + 8 * k, 8), :]


def per_device(gauge_links, in_field, cotangent, bilinear_weights):
    lines = bilinear_weights.shape[2]
    width = lines * C
    f32 = jnp.float32
    gx = ("yhi", "zc")
    n_gx, n_yz, n_zc = lax.axis_size(gx), lax.axis_size("yz"), lax.axis_size("zc")
    swap = lambda v, axes: lax.all_to_all(v, axes, 0, 0, tiled=True)
    spread_over = lambda v, axes: jnp.broadcast_to(v[None], (lax.axis_size(axes),) + v.shape)
    flat = bilinear_weights.reshape(C * C, width)
    weights = jnp.concatenate([jnp.pad(flat, ((0, 0), (0, 8))), jnp.pad(flat, ((0, 0), (8, 0)))], axis=0)
    vmem = lambda *shape: pltpu.VMEM(shape, f32)
    grant = lambda mib: pltpu.CompilerParams(vmem_limit_bytes=mib << 20)
    as_rows = lambda v: jnp.transpose(v, (0, 1, 3, 4, 2, 5)).reshape(-1, 128)
    packed = pl.pallas_call(
        pack_kernel,
        out_shape=jax.ShapeDtypeStruct((32, 4, 640), f32),
        in_specs=[pl.BlockSpec(memory_space=pltpu.HBM)] * 3,
        scratch_shapes=[
            vmem(2, 3, 3, 2, 128),
            vmem(288, 128),
            vmem(288, 128),
            vmem(640, 128),
            pltpu.SemaphoreType.DMA((3,)),
        ],
        compiler_params=pltpu.CompilerParams(vmem_limit_bytes=WHOLE),
        name="pack",
    )(jnp.transpose(gauge_links, (0, 2, 3, 1, 4)), as_rows(in_field), as_rows(cotangent))
    packed, weights = lax.optimization_barrier((swap(packed, gx), weights))
    wide = 18 * 128
    shapes = lambda *dims: jax.ShapeDtypeStruct(dims, f32)
    gw_part, grad_part = pl.pallas_call(
        functools.partial(layer_kernel, lines),
        out_shape=(shapes(n_zc, 64 // n_zc, width), shapes(32, 4, 384)),
        scratch_shapes=[
            vmem(sum(KEPT), wide),
            vmem(640, 128),
            vmem(2, 18, 8, 128),
            vmem(width + 8, wide),
            vmem(128, wide),
            vmem(width + 8, wide),
            vmem(2, 18, 8, 128),
            vmem(2, 18, 8, 128),
        ],
        compiler_params=grant(16),
        cost_estimate=pl.CostEstimate(flops=3 * 10**9, bytes_accessed=4 << 20, transcendentals=0),
        name="layer",
    )(packed, weights)
    both = swap(jnp.concatenate([grad_part[:, :, :288], jnp.concatenate([gw_part] * (n_gx // n_zc))], axis=2), gx)
    total = jnp.sum(swap(spread_over(jnp.sum(both[:, :, 288:], axis=0), "yz"), "yz"), axis=0)
    scale = 1.0 / math.sqrt(100.0 * 2 * n_gx * 128 * n_yz)
    grad_weights = swap(spread_over(total * scale, "zc"), "zc").reshape(C, C, lines, C)
    back = jnp.pad(both[:, :, :288], ((0, 0), (0, 0), (0, 96)))
    grad_field = pl.pallas_call(
        unpack_kernel,
        out_shape=jax.ShapeDtypeStruct((288, 128), f32),
        scratch_shapes=[vmem(384, 128)],
        compiler_params=grant(4),
        name="unpack",
    )(back)
    grad_field = jnp.transpose(grad_field.reshape(C, 2, 3, 3, 2, 128), (0, 1, 4, 2, 3, 5))
    return (grad_field, grad_weights)


def solution(mesh):
    n_gx, n_yz = mesh.devices.shape
    split = jax.sharding.Mesh(mesh.devices.reshape(2, n_gx // 2, n_yz), ("yhi", "zc", "yz"))
    gx = ("yhi", "zc")
    placed = (
        P(gx, None, None, None, "yz"),
        P(None, gx, None, None, None, "yz"),
        P(None, gx, None, None, None, "yz"),
        P(),
    )
    return jax.shard_map(
        per_device,
        mesh=split,
        in_specs=placed,
        out_specs=(P(None, gx, None, None, None, "yz"), P()),
        check_vma=False,
    )
```

```python
import functools
import math

import jax
import jax.numpy as jnp
from jax import lax
from jax.experimental import pallas as pl
from jax.experimental.pallas import tpu as pltpu
from jax.sharding import PartitionSpec as P

C = 8
WHOLE = 67043328
HALF = 320


def comp(ri, a, b):
    return (a * 3 + b) * 2 + ri


def product(left, right, dag_left=False, dag_right=False):
    result = [None] * 18
    for a in range(3):
        for b in range(3):
            real = imag = None
            for k in range(3):
                l_at = (k, a) if dag_left else (a, k)
                r_at = (b, k) if dag_right else (k, b)
                l_re, l_im = left[comp(0, *l_at)], left[comp(1, *l_at)]
                r_re, r_im = right[comp(0, *r_at)], right[comp(1, *r_at)]
                rr, ii = l_re * r_re, l_im * r_im
                ri, ir = l_re * r_im, l_im * r_re
                term_re = rr + ii if dag_left != dag_right else rr - ii
                if not dag_left and not dag_right:
                    term_im = ri + ir
                elif dag_left and not dag_right:
                    term_im = ri - ir
                elif dag_right and not dag_left:
                    term_im = ir - ri
                else:
                    term_im = -(ri + ir)
                real = term_re if real is None else real + term_re
                imag = term_im if imag is None else imag + term_im
            result[comp(0, a, b)] = real
            result[comp(1, a, b)] = imag
    return result


def halves(value):
    high = value.astype(jnp.bfloat16)
    return high, (value - high.astype(jnp.float32)).astype(jnp.bfloat16)


def matmul(left, right, dims):
    left_high, left_low = halves(left)
    right_high, right_low = halves(right)
    dot = functools.partial(lax.dot_general, dimension_numbers=(dims, ((), ())), preferred_element_type=jnp.float32)
    return dot(left_high, right_high) + (dot(left_low, right_high) + dot(left_high, right_low))


def pack_kernel(links_far, field_far, cot_far, out, links, field, cot, rows, sems):
    copies = [
        pltpu.make_async_copy(far, near, sems.at[n])
        for n, (far, near) in enumerate(((field_far, field), (links_far, links), (cot_far, cot)))
    ]
    for copy in copies:
        copy.start()
    copies[0].wait()
    for x in range(2):
        rows[pl.ds(x * HALF + 306, 14), :] = jnp.zeros((14, 128), jnp.float32)
        for k in range(18):
            rows[pl.ds(x * HALF + 8 * k, 8), :] = field[pl.ds(18 * x + k, C, stride=36), :]
    copies[1].wait()
    for x in range(2):
        for k in range(9):
            rows[pl.ds(x * HALF + 288 + 2 * k, 2), :] = links[x, k // 3, k % 3]
    copies[2].wait()
    for x in range(2):
        for k in range(18):
            rows[pl.ds(x * HALF + 144 + 8 * k, 8), :] = cot[pl.ds(18 * x + k, C, stride=36), :]
    for block in range(5):
        turned = rows[pl.ds(128 * block, 128), :].T
        out[:, :, pl.ds(128 * block, 128)] = turned.reshape(32, 4, 128)


KEPT = (128, 24, 16, 16, 16)


def parts_of(state):
    starts = [sum(KEPT[:n]) for n in range(len(KEPT))]
    return [state.at[pl.ds(start, size), :] for start, size in zip(starts, KEPT)]


def tile(ref, which, k):
    return ref[pl.ds(8 * which, 8), pl.ds(128 * k, 128)]


def put(ref, which, k, value):
    ref[pl.ds(8 * which, 8), pl.ds(128 * k, 128)] = value


def fill_windows(lines, wt, wp, windows, entries=range(18)):
    lane = lax.broadcasted_iota(jnp.int32, (C, 128), 1)
    for k in entries:
        for t in range(lines + 1):
            x, m = (t + 1) % 2, (t + 1) // 2
            value = tile(wt, x, k)
            if m:
                value = pltpu.roll(jnp.where(lane < 4 * m, tile(wp, x, k), value), 128 - 4 * m, 1)
            put(windows, t, k, value)


def forward_kernel(lines, packed, gw_out, state, rows, gt, windows):
    pair, frame, gt_kept, wt, wp = parts_of(state)
    shape = (C, 128)
    lane = lax.broadcasted_iota(jnp.int32, shape, 1)
    for block in range(5):
        turned = packed[:, :, pl.ds(128 * block, 128)].reshape(128, 128)
        rows[pl.ds(128 * block, 128), :] = turned.T

    def load8(x, offset):
        return [rows[pl.ds(x * HALF + offset + 8 * k, 8), :] for k in range(18)]

    def load_link(x):
        return [jnp.broadcast_to(rows[pl.ds(x * HALF + 288 + k, 1), :], shape) for k in range(18)]

    one = [jnp.full(shape, 1.0 if k in (0, 8, 16) else 0.0, jnp.float32) for k in range(18)]
    even = load_link(0)
    scan = product(even, load_link(1))
    step = 1
    while step < 32:
        moved = [pltpu.roll(v, 4 * step, 1) for v in scan]
        longer = product(moved, scan)
        scan = [jnp.where(lane >= 4 * step, n, v) for n, v in zip(longer, scan)]
        step *= 2
    for k in range(18):
        before = jnp.where(lane >= 4, pltpu.roll(scan[k], 4, 1), one[k])
        put(frame, 0, k, before)
        whole = scan[k]
        reach = 1
        while reach < 32:
            whole = jnp.where(lane < 128 - 4 * reach, pltpu.roll(whole, 128 - 4 * reach, 1), whole)
            reach *= 2
        put(frame, 2, k, whole)
    def get_frame(which):
        return [tile(frame, which, k) for k in range(18)]

    v_odd = product(get_frame(0), load_link(0))
    for k in range(18):
        put(frame, 1, k, v_odd[k])

    for x in range(2):
        turned = product(product(get_frame(x), load8(x, 144)), get_frame(x), dag_right=True)
        for k in range(18):
            put(gt_kept, x, k, turned[k])
            gt[x, k] = turned[k]
        turned = product(product(get_frame(x), load8(x, 0)), get_frame(x), dag_right=True)
        for k in range(18):
            put(wt, x, k, turned[k])
        turned = product(product(get_frame(2), [tile(wt, x, k) for k in range(18)]), get_frame(2), dag_right=True)
        for k in range(18):
            put(wp, x, k, turned[k])

    for x in range(2):
        for i in range(C):
            value = product([tile(wt, x, k) for k in range(18)], spread(gt, x, i), dag_left=True)
            for k in range(18):
                put(pair, 8 * x + i, k, value[k])
    gw2 = None
    for first in range(0, 18, 2):
        fill_windows(lines, wt, wp, windows, range(first, first + 2))
        columns = pl.ds(128 * first, 128 * 2)
        part = matmul(pair[:, columns], windows[:, columns], ((1,), (1,)))
        gw2 = part if gw2 is None else gw2 + part
    width = lines * C
    gw_out[...] = (gw2[:64, :width] + gw2[64:, 8:8 + width]).reshape(gw_out.shape)


def spread(source, x, i):
    return [jnp.broadcast_to(source[x, k, pl.ds(i, 1), :], (C, 128)) for k in range(18)]


def backward_kernel(lines, weights, state, grad_out, rows, mixed, back, acc, wrap, gt, windows):
    pair, frame, gt_kept, wt, wp = parts_of(state)
    fill_windows(lines, wt, wp, windows)
    for x in range(2):
        for k in range(18):
            gt[x, k] = tile(gt_kept, x, k)
    shape = (C, 128)
    lane = lax.broadcasted_iota(jnp.int32, shape, 1)

    def get_frame(which):
        return [tile(frame, which, k) for k in range(18)]

    for first in range(0, 18, 6):
        columns = pl.ds(128 * first, 128 * 6)
        mixed[:, columns] = matmul(weights[...], windows[:, columns], ((1,), (0,)))
        back[:, columns] = matmul(weights[...], pair[:, columns], ((0,), (0,)))

    for k in range(18):
        columns = pl.ds(128 * k, 128)
        for x in range(2):
            inside = jnp.zeros(shape, jnp.float32)
            wrapped = jnp.zeros(shape, jnp.float32)
            for t in range(lines + 1):
                if (t + 1) % 2 != x:
                    continue
                m = (t + 1) // 2
                value = back[pl.ds(8 * t, 8), columns]
                if m:
                    value = pltpu.roll(value, 4 * m, 1)
                    wrapped = wrapped + jnp.where(lane < 4 * m, value, 0.0)
                    inside = inside + jnp.where(lane < 4 * m, 0.0, value)
                else:
                    inside = inside + value
            acc[x, k] = inside
            wrap[x, k] = wrapped

    for x in range(2):
        turned = product(product(get_frame(2), [wrap[x, k] for k in range(18)], dag_left=True), get_frame(2))
        for k in range(18):
            acc[x, k] = acc[x, k] + turned[k]

        for i in range(C):
            here = [tile(mixed, 8 * x + i, k) for k in range(18)]
            value = product(spread(gt, x, i), here, dag_right=True)
            for k in range(18):
                acc[x, k] = acc[x, k] + value[k]

        turned = product(product(get_frame(x), [acc[x, k] for k in range(18)], dag_left=True), get_frame(x))
        for k in range(18):
            rows[pl.ds(144 * x + 8 * k, 8), :] = turned[k]
    rows[pl.ds(288, 96), :] = jnp.zeros((96, 128), jnp.float32)
    for block in range(3):
        turned = rows[pl.ds(128 * block, 128), :].T
        grad_out[:, :, pl.ds(128 * block, 128)] = turned.reshape(32, 4, 128)


def unpack_kernel(packed, out, rows):
    for block in range(3):
        turned = packed[:, :, pl.ds(128 * block, 128)].reshape(128, 128)
        rows[pl.ds(128 * block, 128), :] = turned.T
    for x in range(2):
        for k in range(18):
            out[pl.ds(18 * x + k, C, stride=36), :] = rows[pl.ds(144 * x + 8 * k, 8), :]


def per_device(gauge_links, in_field, cotangent, bilinear_weights):
    lines = bilinear_weights.shape[2]
    width = lines * C
    f32 = jnp.float32
    gx = ("zy", "core")
    n_gx, n_yz = lax.axis_size(gx), lax.axis_size("yz")
    flat = bilinear_weights.reshape(C * C, width)
    weights = jnp.concatenate([jnp.pad(flat, ((0, 0), (0, 8))), jnp.pad(flat, ((0, 0), (8, 0)))], axis=0)
    vmem = lambda *shape: pltpu.VMEM(shape, f32)
    grant = lambda mib: pltpu.CompilerParams(vmem_limit_bytes=mib << 20)
    as_rows = lambda v: jnp.transpose(v, (0, 1, 3, 4, 2, 5)).reshape(-1, 128)
    packed = pl.pallas_call(
        pack_kernel,
        out_shape=jax.ShapeDtypeStruct((32, 4, 640), f32),
        in_specs=[pl.BlockSpec(memory_space=pltpu.HBM)] * 3,
        scratch_shapes=[
            vmem(2, 3, 3, 2, 128),
            vmem(288, 128),
            vmem(288, 128),
            vmem(640, 128),
            pltpu.SemaphoreType.DMA((3,)),
        ],
        compiler_params=pltpu.CompilerParams(vmem_limit_bytes=WHOLE),
        name="pack",
    )(jnp.transpose(gauge_links, (0, 2, 3, 1, 4)), as_rows(in_field), as_rows(cotangent))
    packed = lax.all_to_all(packed, gx, 0, 0, tiled=True)
    wide = 18 * 128
    shapes = lambda *dims: jax.ShapeDtypeStruct(dims, f32)
    gw_part, state = pl.pallas_call(
        functools.partial(forward_kernel, lines),
        out_shape=(
            shapes(n_yz, 64 // n_yz, width),
            shapes(sum(KEPT), wide),
        ),
        scratch_shapes=[vmem(640, 128), vmem(2, 18, 8, 128), vmem(width + 8, wide)],
        compiler_params=grant(12),
        cost_estimate=pl.CostEstimate(flops=10**9, bytes_accessed=4 << 20, transcendentals=0),
        name="forward",
    )(packed)
    grad_part = pl.pallas_call(
        functools.partial(backward_kernel, lines),
        out_shape=shapes(32, 4, 384),
        scratch_shapes=[
            vmem(384, 128),
            vmem(128, wide),
            vmem(width + 8, wide),
            vmem(2, 18, 8, 128),
            vmem(2, 18, 8, 128),
            vmem(2, 18, 8, 128),
            vmem(width + 8, wide),
        ],
        compiler_params=grant(14),
        cost_estimate=pl.CostEstimate(flops=2 * 10**9, bytes_accessed=4 << 20, transcendentals=0),
        name="backward",
    )(weights, state)
    gw_part = lax.all_to_all(gw_part, "yz", 0, 0, tiled=True)
    gw_part = jnp.sum(gw_part, axis=0)
    half = width // 2
    to_first = lax.broadcasted_iota(jnp.int32, (n_gx, 4, half), 0) % 2 == 0
    for_core = jnp.where(to_first, gw_part[None, :, :half], gw_part[None, :, half:])
    both = jnp.concatenate([grad_part[:, :, :288], for_core], axis=2)
    both = lax.all_to_all(both, gx, 0, 0, tiled=True)
    total = jnp.sum(both[:, :, 288:], axis=0)
    scale = 1.0 / math.sqrt(100.0 * 2 * n_gx * 128 * n_yz)
    total = jnp.broadcast_to((total * scale)[None], (2 * n_yz,) + total.shape)
    total = lax.all_to_all(total, ("core", "yz"), 0, 0, tiled=True)
    total = total.reshape(2, C, C, lines // 2, C)
    grad_weights = jnp.concatenate([total[0], total[1]], axis=2)
    grad_field = pl.pallas_call(
        unpack_kernel,
        out_shape=jax.ShapeDtypeStruct((288, 128), f32),
        scratch_shapes=[vmem(384, 128)],
        compiler_params=grant(4),
        name="unpack",
    )(both)
    grad_field = jnp.transpose(grad_field.reshape(C, 2, 3, 3, 2, 128), (0, 1, 4, 2, 3, 5))
    return (grad_field, grad_weights)


def solution(mesh):
    n_gx, n_yz = mesh.devices.shape
    split = jax.sharding.Mesh(mesh.devices.reshape(n_gx // 2, 2, n_yz), ("zy", "core", "yz"))
    gx = ("zy", "core")
    placed = (
        P(gx, None, None, None, "yz"),
        P(None, gx, None, None, None, "yz"),
        P(None, gx, None, None, None, "yz"),
        P(),
    )
    return jax.shard_map(
        per_device,
        mesh=split,
        in_specs=placed,
        out_specs=(P(None, gx, None, None, None, "yz"), P()),
        check_vma=False,
    )
```

```python
import functools
import math

import jax
import jax.numpy as jnp
from jax import lax
from jax.experimental import pallas as pl
from jax.experimental.pallas import tpu as pltpu
from jax.sharding import PartitionSpec as P

C = 8
WHOLE = 67043328
HALF = 320


def comp(ri, a, b):
    return (a * 3 + b) * 2 + ri


def product(left, right, dag_left=False, dag_right=False):
    result = [None] * 18
    for a in range(3):
        for b in range(3):
            real = imag = None
            for k in range(3):
                l_at = (k, a) if dag_left else (a, k)
                r_at = (b, k) if dag_right else (k, b)
                l_re, l_im = left[comp(0, *l_at)], left[comp(1, *l_at)]
                r_re, r_im = right[comp(0, *r_at)], right[comp(1, *r_at)]
                rr, ii = l_re * r_re, l_im * r_im
                ri, ir = l_re * r_im, l_im * r_re
                term_re = rr + ii if dag_left != dag_right else rr - ii
                if not dag_left and not dag_right:
                    term_im = ri + ir
                elif dag_left and not dag_right:
                    term_im = ri - ir
                elif dag_right and not dag_left:
                    term_im = ir - ri
                else:
                    term_im = -(ri + ir)
                real = term_re if real is None else real + term_re
                imag = term_im if imag is None else imag + term_im
            result[comp(0, a, b)] = real
            result[comp(1, a, b)] = imag
    return result


def halves(value):
    high = value.astype(jnp.bfloat16)
    return high, (value - high.astype(jnp.float32)).astype(jnp.bfloat16)


def matmul(left, right, dims):
    left_high, left_low = halves(left)
    right_high, right_low = halves(right)
    dot = functools.partial(lax.dot_general, dimension_numbers=(dims, ((), ())), preferred_element_type=jnp.float32)
    return dot(left_high, right_high) + (dot(left_low, right_high) + dot(left_high, right_low))


def pack_kernel(links_far, field_far, cot_far, out, links, field, cot, rows, sems):
    copies = [
        pltpu.make_async_copy(far, near, sems.at[n])
        for n, (far, near) in enumerate(((field_far, field), (links_far, links), (cot_far, cot)))
    ]
    for copy in copies:
        copy.start()
    copies[0].wait()
    for x in range(2):
        rows[pl.ds(x * HALF + 306, 14), :] = jnp.zeros((14, 128), jnp.float32)
        for k in range(18):
            rows[pl.ds(x * HALF + 8 * k, 8), :] = field[pl.ds(18 * x + k, C, stride=36), :]
    copies[1].wait()
    for x in range(2):
        for k in range(9):
            rows[pl.ds(x * HALF + 288 + 2 * k, 2), :] = links[x, k // 3, k % 3]
    copies[2].wait()
    for x in range(2):
        for k in range(18):
            rows[pl.ds(x * HALF + 144 + 8 * k, 8), :] = cot[pl.ds(18 * x + k, C, stride=36), :]
    for block in range(5):
        turned = rows[pl.ds(128 * block, 128), :].T
        out[:, :, pl.ds(128 * block, 128)] = turned.reshape(32, 4, 128)


KEPT = (128, 24, 16, 16, 16)


def parts_of(state):
    starts = [sum(KEPT[:n]) for n in range(len(KEPT))]
    return [state.at[pl.ds(start, size), :] for start, size in zip(starts, KEPT)]


def tile(ref, which, k):
    return ref[pl.ds(8 * which, 8), pl.ds(128 * k, 128)]


def put(ref, which, k, value):
    ref[pl.ds(8 * which, 8), pl.ds(128 * k, 128)] = value


def fill_windows(lines, wt, wp, windows, entries=range(18)):
    lane = lax.broadcasted_iota(jnp.int32, (C, 128), 1)
    for k in entries:
        for t in range(lines + 1):
            x, m = (t + 1) % 2, (t + 1) // 2
            value = tile(wt, x, k)
            if m:
                value = pltpu.roll(jnp.where(lane < 4 * m, tile(wp, x, k), value), 128 - 4 * m, 1)
            put(windows, t, k, value)


def forward_kernel(lines, packed, gw_out, state, rows, gt, windows):
    pair, frame, gt_kept, wt, wp = parts_of(state)
    shape = (C, 128)
    lane = lax.broadcasted_iota(jnp.int32, shape, 1)
    for block in range(5):
        turned = packed[:, :, pl.ds(128 * block, 128)].reshape(128, 128)
        rows[pl.ds(128 * block, 128), :] = turned.T

    def load8(x, offset):
        return [rows[pl.ds(x * HALF + offset + 8 * k, 8), :] for k in range(18)]

    def load_link(x):
        return [jnp.broadcast_to(rows[pl.ds(x * HALF + 288 + k, 1), :], shape) for k in range(18)]

    one = [jnp.full(shape, 1.0 if k in (0, 8, 16) else 0.0, jnp.float32) for k in range(18)]
    even = load_link(0)
    scan = product(even, load_link(1))
    step = 1
    while step < 32:
        moved = [pltpu.roll(v, 4 * step, 1) for v in scan]
        longer = product(moved, scan)
        scan = [jnp.where(lane >= 4 * step, n, v) for n, v in zip(longer, scan)]
        step *= 2
    for k in range(18):
        before = jnp.where(lane >= 4, pltpu.roll(scan[k], 4, 1), one[k])
        put(frame, 0, k, before)
        whole = scan[k]
        reach = 1
        while reach < 32:
            whole = jnp.where(lane < 128 - 4 * reach, pltpu.roll(whole, 128 - 4 * reach, 1), whole)
            reach *= 2
        put(frame, 2, k, whole)
    def get_frame(which):
        return [tile(frame, which, k) for k in range(18)]

    v_odd = product(get_frame(0), load_link(0))
    for k in range(18):
        put(frame, 1, k, v_odd[k])

    for x in range(2):
        turned = product(product(get_frame(x), load8(x, 144)), get_frame(x), dag_right=True)
        for k in range(18):
            put(gt_kept, x, k, turned[k])
            gt[x, k] = turned[k]
        turned = product(product(get_frame(x), load8(x, 0)), get_frame(x), dag_right=True)
        for k in range(18):
            put(wt, x, k, turned[k])
        turned = product(product(get_frame(2), [tile(wt, x, k) for k in range(18)]), get_frame(2), dag_right=True)
        for k in range(18):
            put(wp, x, k, turned[k])

    for x in range(2):
        for i in range(C):
            value = product([tile(wt, x, k) for k in range(18)], spread(gt, x, i), dag_left=True)
            for k in range(18):
                put(pair, 8 * x + i, k, value[k])
    gw2 = None
    for first in range(0, 18, 2):
        fill_windows(lines, wt, wp, windows, range(first, first + 2))
        columns = pl.ds(128 * first, 128 * 2)
        part = matmul(pair[:, columns], windows[:, columns], ((1,), (1,)))
        gw2 = part if gw2 is None else gw2 + part
    width = lines * C
    gw_out[...] = (gw2[:64, :width] + gw2[64:, 8:8 + width]).reshape(gw_out.shape)


def spread(source, x, i):
    return [jnp.broadcast_to(source[x, k, pl.ds(i, 1), :], (C, 128)) for k in range(18)]


def backward_kernel(lines, weights, state, grad_out, rows, mixed, back, acc, wrap, gt, windows):
    pair, frame, gt_kept, wt, wp = parts_of(state)
    fill_windows(lines, wt, wp, windows)
    for x in range(2):
        for k in range(18):
            gt[x, k] = tile(gt_kept, x, k)
    shape = (C, 128)
    lane = lax.broadcasted_iota(jnp.int32, shape, 1)

    def get_frame(which):
        return [tile(frame, which, k) for k in range(18)]

    for first in range(0, 18, 6):
        columns = pl.ds(128 * first, 128 * 6)
        mixed[:, columns] = matmul(weights[...], windows[:, columns], ((1,), (0,)))
        back[:, columns] = matmul(weights[...], pair[:, columns], ((0,), (0,)))

    for k in range(18):
        columns = pl.ds(128 * k, 128)
        for x in range(2):
            inside = jnp.zeros(shape, jnp.float32)
            wrapped = jnp.zeros(shape, jnp.float32)
            for t in range(lines + 1):
                if (t + 1) % 2 != x:
                    continue
                m = (t + 1) // 2
                value = back[pl.ds(8 * t, 8), columns]
                if m:
                    value = pltpu.roll(value, 4 * m, 1)
                    wrapped = wrapped + jnp.where(lane < 4 * m, value, 0.0)
                    inside = inside + jnp.where(lane < 4 * m, 0.0, value)
                else:
                    inside = inside + value
            acc[x, k] = inside
            wrap[x, k] = wrapped

    for x in range(2):
        turned = product(product(get_frame(2), [wrap[x, k] for k in range(18)], dag_left=True), get_frame(2))
        for k in range(18):
            acc[x, k] = acc[x, k] + turned[k]

        for i in range(C):
            here = [tile(mixed, 8 * x + i, k) for k in range(18)]
            value = product(spread(gt, x, i), here, dag_right=True)
            for k in range(18):
                acc[x, k] = acc[x, k] + value[k]

        turned = product(product(get_frame(x), [acc[x, k] for k in range(18)], dag_left=True), get_frame(x))
        for k in range(18):
            rows[pl.ds(144 * x + 8 * k, 8), :] = turned[k]
    rows[pl.ds(288, 96), :] = jnp.zeros((96, 128), jnp.float32)
    for block in range(3):
        turned = rows[pl.ds(128 * block, 128), :].T
        grad_out[:, :, pl.ds(128 * block, 128)] = turned.reshape(32, 4, 128)


def unpack_kernel(packed, out, rows):
    for block in range(3):
        turned = packed[:, :, pl.ds(128 * block, 128)].reshape(128, 128)
        rows[pl.ds(128 * block, 128), :] = turned.T
    for x in range(2):
        for k in range(18):
            out[pl.ds(18 * x + k, C, stride=36), :] = rows[pl.ds(144 * x + 8 * k, 8), :]


def per_device(gauge_links, in_field, cotangent, bilinear_weights):
    lines = bilinear_weights.shape[2]
    width = lines * C
    f32 = jnp.float32
    gx = ("zy", "core")
    n_gx, n_yz = lax.axis_size(gx), lax.axis_size("yz")
    flat = bilinear_weights.reshape(C * C, width)
    weights = jnp.concatenate([jnp.pad(flat, ((0, 0), (0, 8))), jnp.pad(flat, ((0, 0), (8, 0)))], axis=0)
    vmem = lambda *shape: pltpu.VMEM(shape, f32)
    grant = lambda mib: pltpu.CompilerParams(vmem_limit_bytes=mib << 20)
    as_rows = lambda v: jnp.transpose(v, (0, 1, 3, 4, 2, 5)).reshape(-1, 128)
    packed = pl.pallas_call(
        pack_kernel,
        out_shape=jax.ShapeDtypeStruct((32, 4, 640), f32),
        in_specs=[pl.BlockSpec(memory_space=pltpu.HBM)] * 3,
        scratch_shapes=[
            vmem(2, 3, 3, 2, 128),
            vmem(288, 128),
            vmem(288, 128),
            vmem(640, 128),
            pltpu.SemaphoreType.DMA((3,)),
        ],
        compiler_params=pltpu.CompilerParams(vmem_limit_bytes=WHOLE),
        name="pack",
    )(jnp.transpose(gauge_links, (0, 2, 3, 1, 4)), as_rows(in_field), as_rows(cotangent))
    packed = lax.all_to_all(packed, gx, 0, 0, tiled=True)
    wide = 18 * 128
    shapes = lambda *dims: jax.ShapeDtypeStruct(dims, f32)
    gw_part, state = pl.pallas_call(
        functools.partial(forward_kernel, lines),
        out_shape=(
            shapes(n_yz, 64 // n_yz, width),
            shapes(sum(KEPT), wide),
        ),
        scratch_shapes=[vmem(640, 128), vmem(2, 18, 8, 128), vmem(width + 8, wide)],
        compiler_params=grant(12),
        cost_estimate=pl.CostEstimate(flops=10**9, bytes_accessed=4 << 20, transcendentals=0),
        name="forward",
    )(packed)
    grad_part = pl.pallas_call(
        functools.partial(backward_kernel, lines),
        out_shape=shapes(32, 4, 384),
        scratch_shapes=[
            vmem(384, 128),
            vmem(128, wide),
            vmem(width + 8, wide),
            vmem(2, 18, 8, 128),
            vmem(2, 18, 8, 128),
            vmem(2, 18, 8, 128),
            vmem(width + 8, wide),
        ],
        compiler_params=grant(14),
        cost_estimate=pl.CostEstimate(flops=2 * 10**9, bytes_accessed=4 << 20, transcendentals=0),
        name="backward",
    )(weights, state)
    gw_part = lax.all_to_all(gw_part, "yz", 0, 0, tiled=True)
    gw_part = jnp.sum(gw_part, axis=0)
    half = width // 2
    to_first = lax.broadcasted_iota(jnp.int32, (n_gx, 4, half), 0) % 2 == 0
    gw_part = gw_part.reshape(8, half)
    for_core = jnp.where(to_first, gw_part[None, :4], gw_part[None, 4:])
    both = jnp.concatenate([grad_part[:, :, :288], for_core], axis=2)
    both = lax.all_to_all(both, gx, 0, 0, tiled=True)
    total = jnp.sum(both[:, :, 288:], axis=0)
    scale = 1.0 / math.sqrt(100.0 * 2 * n_gx * 128 * n_yz)
    total = jnp.broadcast_to((total * scale)[None], (2 * n_yz,) + total.shape)
    grad_weights = lax.all_to_all(total, ("yz", "core"), 0, 0, tiled=True).reshape(C, C, lines, C)
    grad_field = pl.pallas_call(
        unpack_kernel,
        out_shape=jax.ShapeDtypeStruct((288, 128), f32),
        scratch_shapes=[vmem(384, 128)],
        compiler_params=grant(4),
        name="unpack",
    )(both)
    grad_field = jnp.transpose(grad_field.reshape(C, 2, 3, 3, 2, 128), (0, 1, 4, 2, 3, 5))
    return (grad_field, grad_weights)


def solution(mesh):
    n_gx, n_yz = mesh.devices.shape
    split = jax.sharding.Mesh(mesh.devices.reshape(n_gx // 2, 2, n_yz), ("zy", "core", "yz"))
    gx = ("zy", "core")
    placed = (
        P(gx, None, None, None, "yz"),
        P(None, gx, None, None, None, "yz"),
        P(None, gx, None, None, None, "yz"),
        P(),
    )
    return jax.shard_map(
        per_device,
        mesh=split,
        in_specs=placed,
        out_specs=(P(None, gx, None, None, None, "yz"), P()),
        check_vma=False,
    )
```

```python
import functools
import math

import jax
import jax.numpy as jnp
from jax import lax
from jax.experimental import pallas as pl
from jax.experimental.pallas import tpu as pltpu
from jax.sharding import PartitionSpec as P

C = 8
WHOLE = 67043328
HALF = 320


def comp(ri, a, b):
    return (a * 3 + b) * 2 + ri


def product(left, right, dag_left=False, dag_right=False):
    result = [None] * 18
    for a in range(3):
        for b in range(3):
            real = imag = None
            for k in range(3):
                l_at = (k, a) if dag_left else (a, k)
                r_at = (b, k) if dag_right else (k, b)
                l_re, l_im = left[comp(0, *l_at)], left[comp(1, *l_at)]
                r_re, r_im = right[comp(0, *r_at)], right[comp(1, *r_at)]
                rr, ii = l_re * r_re, l_im * r_im
                ri, ir = l_re * r_im, l_im * r_re
                term_re = rr + ii if dag_left != dag_right else rr - ii
                if not dag_left and not dag_right:
                    term_im = ri + ir
                elif dag_left and not dag_right:
                    term_im = ri - ir
                elif dag_right and not dag_left:
                    term_im = ir - ri
                else:
                    term_im = -(ri + ir)
                real = term_re if real is None else real + term_re
                imag = term_im if imag is None else imag + term_im
            result[comp(0, a, b)] = real
            result[comp(1, a, b)] = imag
    return result


def halves(value):
    high = value.astype(jnp.bfloat16)
    return high, (value - high.astype(jnp.float32)).astype(jnp.bfloat16)


def matmul(left, right, dims):
    left_high, left_low = halves(left)
    right_high, right_low = halves(right)
    dot = functools.partial(lax.dot_general, dimension_numbers=(dims, ((), ())), preferred_element_type=jnp.float32)
    return dot(left_high, right_high) + (dot(left_low, right_high) + dot(left_high, right_low))


def pack_kernel(links_far, field_far, cot_far, out_far, links, field, cot, rows, out, sems, out_sems):
    copies = [
        pltpu.make_async_copy(far, near, sems.at[n])
        for n, (far, near) in enumerate(((field_far, field), (links_far, links), (cot_far, cot)))
    ]
    for copy in copies:
        copy.start()
    copies[0].wait()
    for x in range(2):
        rows[pl.ds(x * HALF + 306, 14), :] = jnp.zeros((14, 128), jnp.float32)
        for k in range(18):
            rows[pl.ds(x * HALF + 8 * k, 8), :] = field[pl.ds(18 * x + k, C, stride=36), :]
    copies[1].wait()
    for x in range(2):
        for k in range(9):
            rows[pl.ds(x * HALF + 288 + 2 * k, 2), :] = links[x, k // 3, k % 3]
    copies[2].wait()
    for x in range(2):
        for k in range(18):
            rows[pl.ds(x * HALF + 144 + 8 * k, 8), :] = cot[pl.ds(18 * x + k, C, stride=36), :]
    sent = []
    for block in range(5):
        turned = rows[pl.ds(128 * block, 128), :].T
        out[block] = turned.reshape(32, 4, 128)
        there = out_far.at[:, :, pl.ds(128 * block, 128)]
        sent.append(pltpu.make_async_copy(out.at[block], there, out_sems.at[block]))
        sent[-1].start()
    for copy in sent:
        copy.wait()


KEPT = (128, 24, 16, 16, 16)


def parts_of(state):
    starts = [sum(KEPT[:n]) for n in range(len(KEPT))]
    return [state.at[pl.ds(start, size), :] for start, size in zip(starts, KEPT)]


def tile(ref, which, k):
    return ref[pl.ds(8 * which, 8), pl.ds(128 * k, 128)]


def put(ref, which, k, value):
    ref[pl.ds(8 * which, 8), pl.ds(128 * k, 128)] = value


def fill_windows(lines, wt, wp, windows, entries=range(18)):
    lane = lax.broadcasted_iota(jnp.int32, (C, 128), 1)
    for k in entries:
        for t in range(lines + 1):
            x, m = (t + 1) % 2, (t + 1) // 2
            value = tile(wt, x, k)
            if m:
                value = pltpu.roll(jnp.where(lane < 4 * m, tile(wp, x, k), value), 128 - 4 * m, 1)
            put(windows, t, k, value)


def forward_kernel(lines, packed, gw_out, state, rows, gt, windows):
    pair, frame, gt_kept, wt, wp = parts_of(state)
    shape = (C, 128)
    lane = lax.broadcasted_iota(jnp.int32, shape, 1)
    for block in range(5):
        turned = packed[:, :, pl.ds(128 * block, 128)].reshape(128, 128)
        rows[pl.ds(128 * block, 128), :] = turned.T

    def load8(x, offset):
        return [rows[pl.ds(x * HALF + offset + 8 * k, 8), :] for k in range(18)]

    def load_link(x):
        return [jnp.broadcast_to(rows[pl.ds(x * HALF + 288 + k, 1), :], shape) for k in range(18)]

    one = [jnp.full(shape, 1.0 if k in (0, 8, 16) else 0.0, jnp.float32) for k in range(18)]
    even = load_link(0)
    scan = product(even, load_link(1))
    step = 1
    while step < 32:
        moved = [pltpu.roll(v, 4 * step, 1) for v in scan]
        longer = product(moved, scan)
        scan = [jnp.where(lane >= 4 * step, n, v) for n, v in zip(longer, scan)]
        step *= 2
    for k in range(18):
        before = jnp.where(lane >= 4, pltpu.roll(scan[k], 4, 1), one[k])
        put(frame, 0, k, before)
        whole = scan[k]
        reach = 1
        while reach < 32:
            whole = jnp.where(lane < 128 - 4 * reach, pltpu.roll(whole, 128 - 4 * reach, 1), whole)
            reach *= 2
        put(frame, 2, k, whole)
    def get_frame(which):
        return [tile(frame, which, k) for k in range(18)]

    v_odd = product(get_frame(0), load_link(0))
    for k in range(18):
        put(frame, 1, k, v_odd[k])

    for x in range(2):
        turned = product(product(get_frame(x), load8(x, 144)), get_frame(x), dag_right=True)
        for k in range(18):
            put(gt_kept, x, k, turned[k])
            gt[x, k] = turned[k]
        turned = product(product(get_frame(x), load8(x, 0)), get_frame(x), dag_right=True)
        for k in range(18):
            put(wt, x, k, turned[k])
        turned = product(product(get_frame(2), [tile(wt, x, k) for k in range(18)]), get_frame(2), dag_right=True)
        for k in range(18):
            put(wp, x, k, turned[k])

    for x in range(2):
        for i in range(C):
            value = product([tile(wt, x, k) for k in range(18)], spread(gt, x, i), dag_left=True)
            for k in range(18):
                put(pair, 8 * x + i, k, value[k])
    gw2 = None
    for first in range(0, 18, 2):
        fill_windows(lines, wt, wp, windows, range(first, first + 2))
        columns = pl.ds(128 * first, 128 * 2)
        part = matmul(pair[:, columns], windows[:, columns], ((1,), (1,)))
        gw2 = part if gw2 is None else gw2 + part
    width = lines * C
    gw_out[...] = (gw2[:64, :width] + gw2[64:, 8:8 + width]).reshape(gw_out.shape)


def spread(source, x, i):
    return [jnp.broadcast_to(source[x, k, pl.ds(i, 1), :], (C, 128)) for k in range(18)]


def backward_kernel(lines, weights, state, grad_out, rows, mixed, back, acc, wrap, gt, windows):
    pair, frame, gt_kept, wt, wp = parts_of(state)
    fill_windows(lines, wt, wp, windows)
    for x in range(2):
        for k in range(18):
            gt[x, k] = tile(gt_kept, x, k)
    shape = (C, 128)
    lane = lax.broadcasted_iota(jnp.int32, shape, 1)

    def get_frame(which):
        return [tile(frame, which, k) for k in range(18)]

    for first in range(0, 18, 6):
        columns = pl.ds(128 * first, 128 * 6)
        mixed[:, columns] = matmul(weights[...], windows[:, columns], ((1,), (0,)))
        back[:, columns] = matmul(weights[...], pair[:, columns], ((0,), (0,)))

    for k in range(18):
        columns = pl.ds(128 * k, 128)
        for x in range(2):
            inside = jnp.zeros(shape, jnp.float32)
            wrapped = jnp.zeros(shape, jnp.float32)
            for t in range(lines + 1):
                if (t + 1) % 2 != x:
                    continue
                m = (t + 1) // 2
                value = back[pl.ds(8 * t, 8), columns]
                if m:
                    value = pltpu.roll(value, 4 * m, 1)
                    wrapped = wrapped + jnp.where(lane < 4 * m, value, 0.0)
                    inside = inside + jnp.where(lane < 4 * m, 0.0, value)
                else:
                    inside = inside + value
            acc[x, k] = inside
            wrap[x, k] = wrapped

    for x in range(2):
        turned = product(product(get_frame(2), [wrap[x, k] for k in range(18)], dag_left=True), get_frame(2))
        for k in range(18):
            acc[x, k] = acc[x, k] + turned[k]

        for i in range(C):
            here = [tile(mixed, 8 * x + i, k) for k in range(18)]
            value = product(spread(gt, x, i), here, dag_right=True)
            for k in range(18):
                acc[x, k] = acc[x, k] + value[k]

        turned = product(product(get_frame(x), [acc[x, k] for k in range(18)], dag_left=True), get_frame(x))
        for k in range(18):
            rows[pl.ds(144 * x + 8 * k, 8), :] = turned[k]
    rows[pl.ds(288, 96), :] = jnp.zeros((96, 128), jnp.float32)
    for block in range(3):
        turned = rows[pl.ds(128 * block, 128), :].T
        grad_out[:, :, pl.ds(128 * block, 128)] = turned.reshape(32, 4, 128)


def unpack_kernel(packed, out, rows):
    for block in range(3):
        turned = packed[:, :, pl.ds(128 * block, 128)].reshape(128, 128)
        rows[pl.ds(128 * block, 128), :] = turned.T
    for x in range(2):
        for k in range(18):
            out[pl.ds(18 * x + k, C, stride=36), :] = rows[pl.ds(144 * x + 8 * k, 8), :]


def per_device(gauge_links, in_field, cotangent, bilinear_weights):
    lines = bilinear_weights.shape[2]
    width = lines * C
    f32 = jnp.float32
    n_gx, n_yz = lax.axis_size("gx"), lax.axis_size("yz")
    flat = bilinear_weights.reshape(C * C, width)
    weights = jnp.concatenate([jnp.pad(flat, ((0, 0), (0, 8))), jnp.pad(flat, ((0, 0), (8, 0)))], axis=0)
    vmem = lambda *shape: pltpu.VMEM(shape, f32)
    grant = lambda mib: pltpu.CompilerParams(vmem_limit_bytes=mib << 20)
    as_rows = lambda v: jnp.transpose(v, (0, 1, 3, 4, 2, 5)).reshape(-1, 128)
    packed = pl.pallas_call(
        pack_kernel,
        out_shape=jax.ShapeDtypeStruct((32, 4, 640), f32),
        in_specs=[pl.BlockSpec(memory_space=pltpu.HBM)] * 3,
        out_specs=pl.BlockSpec(memory_space=pltpu.HBM),
        scratch_shapes=[
            vmem(2, 3, 3, 2, 128),
            vmem(288, 128),
            vmem(288, 128),
            vmem(640, 128),
            vmem(5, 32, 4, 128),
            pltpu.SemaphoreType.DMA((3,)),
            pltpu.SemaphoreType.DMA((5,)),
        ],
        compiler_params=pltpu.CompilerParams(vmem_limit_bytes=WHOLE),
        name="pack",
    )(jnp.transpose(gauge_links, (0, 2, 3, 1, 4)), as_rows(in_field), as_rows(cotangent))
    packed = lax.all_to_all(packed, "gx", 0, 0, tiled=True)
    wide = 18 * 128
    shapes = lambda *dims: jax.ShapeDtypeStruct(dims, f32)
    gw_part, state = pl.pallas_call(
        functools.partial(forward_kernel, lines),
        out_shape=(
            shapes(n_yz, 64 // n_yz, width),
            shapes(sum(KEPT), wide),
        ),
        scratch_shapes=[vmem(640, 128), vmem(2, 18, 8, 128), vmem(width + 8, wide)],
        compiler_params=grant(12),
        cost_estimate=pl.CostEstimate(flops=10**9, bytes_accessed=4 << 20, transcendentals=0),
        name="forward",
    )(packed)
    grad_part = pl.pallas_call(
        functools.partial(backward_kernel, lines),
        out_shape=shapes(32, 4, 384),
        scratch_shapes=[
            vmem(384, 128),
            vmem(128, wide),
            vmem(width + 8, wide),
            vmem(2, 18, 8, 128),
            vmem(2, 18, 8, 128),
            vmem(2, 18, 8, 128),
            vmem(width + 8, wide),
        ],
        compiler_params=grant(14),
        cost_estimate=pl.CostEstimate(flops=2 * 10**9, bytes_accessed=4 << 20, transcendentals=0),
        name="backward",
    )(weights, state)
    gw_part = lax.all_to_all(gw_part, "yz", 0, 0, tiled=True)
    gw_part = jnp.sum(gw_part, axis=0)
    both = jnp.concatenate([grad_part[:, :, :288], jnp.broadcast_to(gw_part[None], (n_gx,) + gw_part.shape)], axis=2)
    both = lax.all_to_all(both, "gx", 0, 0, tiled=True)
    total = jnp.sum(both[:, :, 288:], axis=0)
    scale = 1.0 / math.sqrt(100.0 * 2 * n_gx * 128 * n_yz)
    total = jnp.broadcast_to((total * scale)[None], (n_yz,) + total.shape)
    grad_weights = lax.all_to_all(total, "yz", 0, 0, tiled=True).reshape(C, C, lines, C)
    back = jnp.pad(both[:, :, :288], ((0, 0), (0, 0), (0, 96)))
    grad_field = pl.pallas_call(
        unpack_kernel,
        out_shape=jax.ShapeDtypeStruct((288, 128), f32),
        scratch_shapes=[vmem(384, 128)],
        compiler_params=grant(4),
        name="unpack",
    )(back)
    grad_field = jnp.transpose(grad_field.reshape(C, 2, 3, 3, 2, 128), (0, 1, 4, 2, 3, 5))
    return (grad_field, grad_weights)


def solution(mesh):
    placed = (
        P("gx", None, None, None, "yz"),
        P(None, "gx", None, None, None, "yz"),
        P(None, "gx", None, None, None, "yz"),
        P(),
    )
    return jax.shard_map(
        per_device,
        mesh=mesh,
        in_specs=placed,
        out_specs=(P(None, "gx", None, None, None, "yz"), P()),
        check_vma=False,
    )
```
